128 devices in a mesh: seq: 32 (over y, z, x_lo), head: 4 (over x_hi, core).
Axes of the slice: x: 4 (x_hi: 2, x_lo: 2; x = x_hi * 2 + x_lo), y: 4, z: 4, core: 2. Of those that a mesh axis runs over, the one named last changes fastest.
Arguments:
- query: bfloat16 [16384, 4096], P('seq', 'head'), may hold values from -46 to 46
- key_rows: bfloat16 [16384, 256], P('seq'), may hold values from -6 to 6
- value_rows: bfloat16 [16384, 256], P('seq'), may hold values from -6 to 6
- grad_out: bfloat16 [16384, 4096], P('seq', 'head'), may hold values from -6 to 6
Outputs:
- grad_query: bfloat16 [16384, 4096], P('seq', 'head')
- grad_key: float32 [16384, 256], P('seq')
- grad_value: float32 [16384, 256], P('seq')
The draws below stay inside these ranges and needn't reach their ends.
All inputs are finite; a program needn't handle non-finite values.
Results may differ from the reference program's by a relative error of at most 0.0051.
Values may be sent and summed in bfloat16 or wider, within the bound.
A program may use at most 128 MiB of HBM per device.

```python
import jax
import jax.numpy as jnp
from jax import lax

H = 16
DH = 256
WINDOW = 2048
TOK_DEV = 512
TOKENS = 16384


def shared_keys(key):
    base = jax.random.normal(jax.random.fold_in(key, 11), (TOKENS, DH), jnp.float32)
    return jnp.clip(base, -6.0, 6.0)


def draw_key_rows(key, part):
    return shared_keys(key).astype(jnp.bfloat16)


def draw_query(key, part):
    base = jax.random.normal(jax.random.fold_in(key, 21), (TOKENS, H * DH), jnp.float32)
    base = jnp.clip(base, -6.0, 6.0)
    return base.astype(jnp.bfloat16)


def level_of(key, shape, split, least, top_value):
    loudness, own = 1.0, jax.random.fold_in(key, 6)
    for dim, shards_of in split:
        draws = jnp.exp(jax.random.uniform(jax.random.fold_in(own, dim), (shards_of,), jnp.float32, least / len(split), top_value / len(split)))
        loudness = loudness * jnp.repeat(draws, shape[dim] // shards_of).reshape([-1 if axis == dim else 1 for axis in range(len(shape))])
    return loudness


def bell_draw(own_key, shape, scale, most, split=(), kind=jnp.bfloat16):
    array = scale * jax.random.normal(own_key, shape, jnp.float32)
    if split:
        array = array * level_of(own_key, shape, split, -0.22, 0.18)
    return jnp.clip(array, -most, most).astype(kind)


def setup_inputs(seed: int = 0) -> dict:
    key_list = jax.random.split(jax.random.key(seed), 5)
    query = draw_query(jax.random.fold_in(key_list[4], 71), 0)
    key_rows = draw_key_rows(jax.random.fold_in(key_list[4], 71), 0)
    value_rows = bell_draw(key_list[2], (TOKENS, DH), 1.0, 6.0, ((0, 32),))
    grad_out = bell_draw(key_list[3], (TOKENS, H * DH), 1.0, 6.0, ((0, 32), (1, 4)))
    return dict(query=query, key_rows=key_rows, value_rows=value_rows, grad_out=grad_out)


def reference(query, key_rows, value_rows, grad_out):
    total_rows = query.shape[0]
    head_dim = key_rows.shape[1]
    heads = query.shape[1] // head_dim
    score_scale = head_dim ** -0.5
    block_rows = min(512, TOK_DEV)
    queries = query.reshape(total_rows, heads, head_dim).astype(jnp.float32)
    grads = grad_out.reshape(total_rows, heads, head_dim).astype(jnp.float32)
    zero_rows = jnp.zeros((WINDOW, head_dim), jnp.float32)
    keys_padded = jnp.concatenate([zero_rows, key_rows.astype(jnp.float32)], axis=0)
    values_padded = jnp.concatenate([zero_rows, value_rows.astype(jnp.float32)], axis=0)
    row_ids = jnp.arange(block_rows, dtype=jnp.int32)
    col_ids = jnp.arange(WINDOW + block_rows, dtype=jnp.int32)
    high = lax.Precision.HIGHEST

    def step(carry, index_block):
        dk_acc, dv_acc = carry
        first_row = (index_block * block_rows).astype(jnp.int32)
        q_blk = lax.dynamic_slice_in_dim(queries, first_row, block_rows, 0)
        g_blk = lax.dynamic_slice_in_dim(grads, first_row, block_rows, 0)
        k_blk = lax.dynamic_slice_in_dim(keys_padded, first_row, WINDOW + block_rows, 0)
        v_blk = lax.dynamic_slice_in_dim(values_padded, first_row, WINDOW + block_rows, 0)
        key_pos = first_row - WINDOW + col_ids
        query_pos = first_row + row_ids
        gap_rows = query_pos[:, None] - key_pos[None, :]
        allowed = (gap_rows >= 0) & (gap_rows < WINDOW) & (key_pos >= 0)[None, :]
        scores = jnp.einsum('rhd,cd->hrc', q_blk, k_blk, precision=high) * score_scale
        scores = jnp.where(allowed[None], scores, -jnp.inf)
        row_max = jnp.max(scores, axis=-1, keepdims=True)
        expo = jnp.exp(scores - row_max)
        probs = expo / jnp.sum(expo, axis=-1, keepdims=True)
        probs_low = lax.optimization_barrier(probs.astype(jnp.bfloat16)).astype(jnp.float32)
        dv_blk = jnp.einsum('hrc,rhd->cd', probs_low, g_blk, precision=high)
        dprobs = jnp.einsum('rhd,cd->hrc', g_blk, v_blk, precision=high)
        delta = jnp.sum(probs * dprobs, axis=-1, keepdims=True)
        dscores = (probs * (dprobs - delta) * score_scale).astype(jnp.bfloat16)
        dscores = lax.optimization_barrier(dscores).astype(jnp.float32)
        dq_blk = jnp.einsum('hrc,cd->rhd', dscores, k_blk, precision=high).astype(jnp.bfloat16)
        dk_blk = jnp.einsum('hrc,rhd->cd', dscores, q_blk, precision=high)
        old_k = lax.dynamic_slice_in_dim(dk_acc, first_row, WINDOW + block_rows, 0)
        old_v = lax.dynamic_slice_in_dim(dv_acc, first_row, WINDOW + block_rows, 0)
        dk_acc = lax.dynamic_update_slice_in_dim(dk_acc, old_k + dk_blk, first_row, 0)
        dv_acc = lax.dynamic_update_slice_in_dim(dv_acc, old_v + dv_blk, first_row, 0)
        return (dk_acc, dv_acc), dq_blk.reshape(block_rows, heads * head_dim)

    start_acc = jnp.zeros((total_rows + WINDOW, head_dim), jnp.float32)
    blocks = jnp.arange(total_rows // block_rows, dtype=jnp.int32)
    (dk_acc, dv_acc), dq_all = lax.scan(step, (start_acc, start_acc), blocks)
    grad_query = dq_all.reshape(total_rows, heads * head_dim)
    return grad_query, dk_acc[WINDOW:], dv_acc[WINDOW:]
```

```python
import jax
import jax.numpy as jnp
from jax import lax
from jax.experimental import pallas as pl
from jax.experimental.pallas import tpu as pltpu
from jax.sharding import PartitionSpec as P

F32 = jnp.float32
BF16 = jnp.bfloat16
MESH = pl.DeviceIdType.MESH
REACH = 4
LOG2E = 1.4426950408889634
NEG = -1e30
NT = (((1,), (1,)), ((), ()))
NN = (((1,), (0,)), ((), ()))
TN = (((0,), (0,)), ((), ()))


def kernel(
    q_hbm, g_hbm, k_hbm, v_hbm,
    dq_out, fin_out,
    q_ref, g_ref, kv, e_ref, dp_ref, md, m_run, l_run, dl_run, ds_low, dq_acc,
    acc, pair_send, pair_recv, half_keep, half_send, half_recv,
    quart_send, quart_recv, own_quart, fin,
    load_sem, send_sem, net_sem, mate_sem, pair_sem, half_sem, quart_sem, fin_sem,
):
    tok, dh = kv.shape[2], kv.shape[3]
    heads = e_ref.shape[1]
    hb = tok // 2
    scale = dh ** (-0.5)
    to_log2 = scale * LOG2E
    n_seq = lax.axis_size("seq")
    s, hd = lax.axis_index("seq"), lax.axis_index("head")
    xl, xh, c = lax.rem(s, 2), lax.div(hd, 2), lax.rem(hd, 2)
    opp = s + 1 - 2 * xl
    mate = (s, hd + 1 - 2 * c)
    across = (s, lax.rem(hd + 2, 4))

    def half(index):
        return pl.ds(pl.multiple_of(index * hb, hb), hb)

    loads = [
        pltpu.make_async_copy(src, dst, load_sem.at[i])
        for i, (src, dst) in enumerate(
            ((k_hbm, kv.at[0, 0]), (v_hbm, kv.at[0, 1]), (q_hbm, q_ref), (g_hbm, g_ref))
        )
    ]
    for load in loads:
        load.start()
    barrier = pltpu.get_barrier_semaphore()

    def greet(device):
        pl.semaphore_signal(barrier, inc=1, device_id=device, device_id_type=MESH)

    for head in (hd, across[1]):
        greet((opp, head))
    greet(mate)
    greet(across)
    for d in range(1, REACH + 1):
        @pl.when(s + d < n_seq)
        def _(d=d):
            greet((s + d, hd))

        @pl.when(s >= d)
        def _(d=d):
            greet((s - d, hd))
    ahead = jnp.minimum(n_seq - 1 - s, REACH)
    behind = jnp.minimum(s, REACH)
    pl.semaphore_wait(barrier, 4 + ahead + behind)
    for load in loads:
        load.wait()

    pending = []

    def send(cond, src, dst, recv_sem, device):
        copy = pltpu.make_async_remote_copy(
            src_ref=src, dst_ref=dst, send_sem=send_sem.at[len(pending)], recv_sem=recv_sem,
            device_id=device, device_id_type=MESH,
        )
        pending.append((cond, copy))

        @pl.when(cond)
        def _():
            copy.start()

    def arrived(buf, sem):
        pltpu.make_async_remote_copy(
            src_ref=buf, dst_ref=buf, send_sem=send_sem.at[0], recv_sem=sem,
            device_id=mate, device_id_type=MESH,
        ).wait_recv()

    def when_arrived(cond, buf, sem):
        @pl.when(cond)
        def _():
            arrived(buf, sem)

    def kv_half(d, array, index):
        return kv.at[d, array, half(index), :]

    def over_x(cond, src_slot, dst_slot):
        for x_hi in range(2):
            send(
                cond, kv_half(src_slot, c, xh), kv_half(dst_slot, c, xh), net_sem.at[dst_slot, xh],
                (opp, 2 * x_hi + c),
            )

    def to_mate(cond, d, index):
        send(cond, kv_half(d, c, index), kv_half(d, c, index), mate_sem.at[d, index], mate)

    order = (xh, 1 - xh)
    for index in order:
        send(s + 2 < n_seq, kv_half(0, c, index), kv_half(2, c, index), net_sem.at[2, index], (s + 2, hd))
        if index is order[0]:
            over_x(xl == 0, 0, 1)

    def relay_two(j):
        index = order[j]
        when_arrived(s >= 2, kv_half(2, c, index), net_sem.at[2, index])
        send(
            (s >= 2) & (s + 2 < n_seq), kv_half(2, c, index), kv_half(4, c, index), net_sem.at[4, index],
            (s + 2, hd),
        )
        if j == 0:
            over_x(s >= 2, 2, 3 - 2 * xl)
        to_mate(s >= 2, 2, index)

    def relay_four(j):
        index = order[j]
        when_arrived(s >= 4, kv_half(4, c, index), net_sem.at[4, index])
        if j == 0:
            over_x((s >= 4) & (xl == 1), 4, 3)
        to_mate(s >= 4, 4, index)

    def relay_odd(cond, d):
        for index in range(2):
            when_arrived(cond, kv_half(d, c, index), net_sem.at[d, index])
            to_mate(cond, d, index)

    def mate_ready(d):
        for index in range(2):
            arrived(kv_half(d, 1 - c, index), mate_sem.at[d, index])

    def key_range(d, qc):
        if d == 0:
            return 0, hb * (qc + 1)
        if d == REACH:
            return hb * qc, tok
        return 0, tok

    def query_range(d, kc):
        if d == 0:
            return hb * kc, tok
        if d == REACH:
            return 0, hb * (kc + 1)
        return 0, tok

    def scores_of(d):
        def body(h, carry):
            cols = pl.ds(pl.multiple_of(h * dh, dh), dh)
            for qc in range(2):
                k0, k1 = key_range(d if isinstance(d, int) else 1, qc)
                qs = slice(qc * hb, (qc + 1) * hb)
                logits = to_log2 * lax.dot_general(
                    kv[d, 0, k0:k1, :], q_ref[qs, cols], NT, preferred_element_type=F32
                )
                dprobs = lax.dot_general(
                    kv[d, 1, k0:k1, :], g_ref[qs, cols], NT, preferred_element_type=F32
                )
                first = isinstance(d, int) and d == 0
                if isinstance(d, int):
                    row = lax.broadcasted_iota(jnp.int32, logits.shape, 0) + k0
                    col = lax.broadcasted_iota(jnp.int32, logits.shape, 1) + qc * hb
                    logits = jnp.where((row <= col) if d == 0 else (row > col), logits, NEG)
                top = jnp.max(logits, axis=0, keepdims=True)
                if not first:
                    before = m_run[h, :, qs]
                    top = jnp.maximum(before, top)
                expo = jnp.exp2(logits - top)
                total = jnp.sum(expo, axis=0, keepdims=True)
                dots = jnp.sum(expo * dprobs, axis=0, keepdims=True)
                e_ref[d, h, k0:k1, qs] = expo
                dp_ref[d, h, k0:k1, qs] = dprobs
                md[d, h, :, qs] = top
                if not first:
                    fade = jnp.exp2(before - top)
                    total += l_run[h, :, qs] * fade
                    dots += dl_run[h, :, qs] * fade
                m_run[h, :, qs] = top
                l_run[h, :, qs] = total
                dl_run[h, :, qs] = dots
            return carry

        lax.fori_loop(0, heads, body, 0)

    scores_of(0)
    dq_acc[...] = jnp.zeros_like(dq_acc)
    relay_two(0)
    relay_odd(xl == 1, 1)

    @pl.when(xl == 1)
    def _():
        mate_ready(1)
        scores_of(s * 0 + 1)

    relay_two(1)
    odd_second = 1 + 2 * xl
    relay_odd(s >= odd_second, odd_second)

    @pl.when(s >= 2)
    def _():
        mate_ready(2)
        scores_of(s * 0 + 2)

    relay_four(0)

    @pl.when(s >= odd_second)
    def _():
        mate_ready(odd_second)
        scores_of(odd_second)

    relay_four(1)

    @pl.when(s >= 4)
    def _():
        mate_ready(4)
        scores_of(4)

    relay_odd((xl == 0) & (s >= 4), 3)

    @pl.when((xl == 0) & (s >= 4))
    def _():
        mate_ready(3)
        scores_of(s * 0 + 3)

    inverse = 1.0 / l_run[...]
    dl_run[...] = dl_run[...] * inverse
    l_run[...] = inverse

    def grads_of(d, into):
        static = isinstance(d, int)
        acc[into] = jnp.zeros_like(acc[into])

        def body(h, carry):
            cols = pl.ds(pl.multiple_of(h * dh, dh), dh)
            weight = jnp.exp2(md[d, h] - m_run[h]) * l_run[h]
            delta = dl_run[h]
            for kc in range(2):
                q0, q1 = query_range(d if static else 1, kc)
                ks, qs = slice(kc * hb, (kc + 1) * hb), slice(q0, q1)
                probs = e_ref[d, h, ks, qs] * weight[:, q0:q1]
                dscores = probs * (dp_ref[d, h, ks, qs] - delta[:, q0:q1])
                probs_low, dscores_low = probs.astype(BF16), dscores.astype(BF16)
                ds_low[ks, qs] = dscores_low
                acc[into, 1, ks, :] += lax.dot_general(
                    probs_low, g_ref[qs, cols], NN, preferred_element_type=F32
                )
                acc[into, 0, ks, :] += lax.dot_general(
                    dscores_low, q_ref[qs, cols], NN, preferred_element_type=F32
                )
            for qc in range(2):
                k0, k1 = key_range(d if static else 1, qc)
                qs = slice(qc * hb, (qc + 1) * hb)
                dq_acc[h, qs, :] += lax.dot_general(
                    ds_low[k0:k1, qs], kv[d, 0, k0:k1, :], TN, preferred_element_type=F32
                )
            return carry

        lax.fori_loop(0, heads, body, 0)
        acc[into, 0] = acc[into, 0] * scale

    def pair_out(d):
        @pl.when(s >= d)
        def _():
            pair_send[d] = acc[d % 2, 1 - c].astype(BF16)

        send(s >= d, pair_send.at[d], pair_recv.at[d], pair_sem.at[d], mate)

    def half_out(d):
        @pl.when(s >= d)
        def _():
            arrived(pair_recv.at[d], pair_sem.at[d])
            there, here = half(1 - xh), half(xh)
            half_send[d] = (acc[d % 2, c, there, :] + pair_recv[d, there, :].astype(F32)).astype(BF16)
            half_keep[d] = acc[d % 2, c, here, :] + pair_recv[d, here, :].astype(F32)

        send(s >= d, half_send.at[d], half_recv.at[d], half_sem.at[d], across)

    def quarter_out(d):
        @pl.when(s >= d)
        def _():
            arrived(half_recv.at[d], half_sem.at[d])
            mine = half_keep[d] + half_recv[d].astype(F32)
            if d:
                quart_send[d - 1] = mine.astype(BF16)
            else:
                own_quart[...] = mine

        if d:
            send(s >= d, quart_send.at[d - 1], quart_recv.at[d - 1], quart_sem.at[d - 1], (s - d, hd))

    for d in range(REACH, -1, -1):
        @pl.when(s >= d)
        def _(d=d):
            grads_of(d if d in (0, REACH) else s * 0 + d, d % 2)

        pair_out(d)
        if d + 1 <= REACH:
            half_out(d + 1)
        if d + 2 <= REACH:
            quarter_out(d + 2)
    for h in range(heads):
        dq_out[:, h * dh : (h + 1) * dh] = (dq_acc[h] * scale).astype(BF16)
    half_out(0)
    quarter_out(1)
    quarter_out(0)
    for d in range(REACH, 0, -1):
        @pl.when(s + d < n_seq)
        def _(d=d):
            arrived(quart_recv.at[d - 1], quart_sem.at[d - 1])
            own_quart[...] += quart_recv[d - 1].astype(F32)

    def fin_half(array, index):
        return fin.at[array, half(index), :]

    fin[c, half(xh), :] = own_quart[...].astype(BF16)
    always = s >= 0
    send(always, fin_half(c, xh), fin_half(c, xh), fin_sem.at[0], across)
    send(always, fin_half(c, xh), fin_half(c, xh), fin_sem.at[1], mate)
    arrived(fin_half(c, 1 - xh), fin_sem.at[0])
    send(always, fin_half(c, 1 - xh), fin_half(c, 1 - xh), fin_sem.at[2], mate)
    arrived(fin_half(1 - c, xh), fin_sem.at[1])
    arrived(fin_half(1 - c, 1 - xh), fin_sem.at[2])
    fin_out[...] = fin[...]
    for cond, copy in pending:
        @pl.when(cond)
        def _(copy=copy):
            copy.wait_send()


def on_device(query, key_rows, value_rows, grad_out):
    tok, dh = key_rows.shape
    heads = query.shape[1] // dh
    blocks = REACH + 1
    vmem = pltpu.VMEM
    dma = pltpu.SemaphoreType.DMA
    grad_query, fin = pl.pallas_call(
        kernel,
        out_shape=(
            jax.ShapeDtypeStruct(query.shape, BF16),
            jax.ShapeDtypeStruct((2, tok, dh), BF16),
        ),
        in_specs=[pl.BlockSpec(memory_space=pl.ANY)] * 4,
        out_specs=(pl.BlockSpec(memory_space=vmem),) * 2,
        scratch_shapes=[
            vmem((tok, heads * dh), BF16),
            vmem((tok, heads * dh), BF16),
            vmem((blocks, 2, tok, dh), BF16),
            vmem((blocks, heads, tok, tok), F32),
            vmem((blocks, heads, tok, tok), F32),
            vmem((blocks, heads, 1, tok), F32),
            vmem((heads, 1, tok), F32),
            vmem((heads, 1, tok), F32),
            vmem((heads, 1, tok), F32),
            vmem((tok, tok), BF16),
            vmem((heads, tok, dh), F32),
            vmem((2, 2, tok, dh), F32),
            vmem((blocks, tok, dh), BF16),
            vmem((blocks, tok, dh), BF16),
            vmem((blocks, tok // 2, dh), F32),
            vmem((blocks, tok // 2, dh), BF16),
            vmem((blocks, tok // 2, dh), BF16),
            vmem((REACH, tok // 2, dh), BF16),
            vmem((REACH, tok // 2, dh), BF16),
            vmem((tok // 2, dh), F32),
            vmem((2, tok, dh), BF16),
            dma((4,)),
            dma((64,)),
            dma((blocks, 2)),
            dma((blocks, 2)),
            dma((blocks,)),
            dma((blocks,)),
            dma((REACH,)),
            dma((3,)),
        ],
        compiler_params=pltpu.CompilerParams(
            collective_id=0, has_side_effects=True, vmem_limit_bytes=67043328
        ),
    )(query, grad_out, key_rows, value_rows)
    return grad_query, fin[0].astype(F32), fin[1].astype(F32)


def solution(mesh):
    return jax.shard_map(
        on_device,
        mesh=mesh,
        in_specs=(P("seq", "head"), P("seq", None), P("seq", None), P("seq", "head")),
        out_specs=(P("seq", "head"), P("seq", None), P("seq", None)),
        check_vma=False,
    )
```

```python
import jax
import jax.numpy as jnp
from jax import lax
from jax.experimental import pallas as pl
from jax.experimental.pallas import tpu as pltpu
from jax.sharding import PartitionSpec as P

F32 = jnp.float32
BF16 = jnp.bfloat16
MESH = pl.DeviceIdType.MESH
REACH = 4
LOG2E = 1.4426950408889634
NEG = -1e30
NT = (((1,), (1,)), ((), ()))
NN = (((1,), (0,)), ((), ()))
TN = (((0,), (0,)), ((), ()))


def kernel(
    q_hbm, g_hbm, k_hbm, v_hbm,
    dq_out, fin_out,
    q_ref, g_ref, kv, e_ref, ds_ref, md, m_run, l_run, dl_run, dq_ref,
    acc, pair_send, pair_recv, half_keep, half_send, half_recv,
    quart_send, quart_recv, own_quart, fin,
    load_sem, send_sem, net_sem, mate_sem, pair_sem, half_sem, quart_sem, fin_sem,
):
    tok, dh = e_ref.shape[2], kv.shape[2]
    heads = e_ref.shape[1]
    hb = tok // 2
    blocks = REACH + 1
    scale = dh ** (-0.5)
    to_log2 = scale * LOG2E
    n_seq = lax.axis_size("seq")
    s, hd = lax.axis_index("seq"), lax.axis_index("head")
    xl, xh, c = lax.rem(s, 2), lax.div(hd, 2), lax.rem(hd, 2)
    opp = s + 1 - 2 * xl
    mate = (s, hd + 1 - 2 * c)
    across = (s, lax.rem(hd + 2, 4))

    def half(index):
        return pl.ds(pl.multiple_of(index * hb, hb), hb)

    loads = [
        pltpu.make_async_copy(src, dst, load_sem.at[i])
        for i, (src, dst) in enumerate(
            ((k_hbm, kv.at[0, :tok]), (v_hbm, kv.at[1, :tok]), (q_hbm, q_ref), (g_hbm, g_ref))
        )
    ]
    for load in loads:
        load.start()
    barrier = pltpu.get_barrier_semaphore()

    def greet(device):
        pl.semaphore_signal(barrier, inc=1, device_id=device, device_id_type=MESH)

    for head in (hd, across[1]):
        greet((opp, head))
    greet(mate)
    greet(across)
    for d in range(1, REACH + 1):
        @pl.when(s + d < n_seq)
        def _(d=d):
            greet((s + d, hd))

        @pl.when(s >= d)
        def _(d=d):
            greet((s - d, hd))
    ahead = jnp.minimum(n_seq - 1 - s, REACH)
    behind = jnp.minimum(s, REACH)
    pl.semaphore_wait(barrier, 4 + ahead + behind)
    for load in loads:
        load.wait()

    pending = []

    def send(cond, src, dst, recv_sem, device):
        sem = send_sem.at[len(pending)]
        pending.append((cond, src.shape[0]))

        @pl.when(cond())
        def _():
            pltpu.make_async_remote_copy(
                src_ref=src, dst_ref=dst, send_sem=sem, recv_sem=recv_sem,
                device_id=device, device_id_type=MESH,
            ).start()

    def wait_sent():
        for i, (cond, size) in enumerate(pending):
            @pl.when(cond())
            def _(i=i, size=size):
                buf = pair_send.at[0, :size]
                pltpu.make_async_remote_copy(
                    src_ref=buf, dst_ref=buf, send_sem=send_sem.at[i], recv_sem=fin_sem.at[0],
                    device_id=mate, device_id_type=MESH,
                ).wait_send()

    def arrived(buf, sem):
        pltpu.make_async_remote_copy(
            src_ref=buf, dst_ref=buf, send_sem=send_sem.at[0], recv_sem=sem,
            device_id=mate, device_id_type=MESH,
        ).wait_recv()

    def when_arrived(cond, buf, sem):
        @pl.when(cond())
        def _():
            arrived(buf, sem)

    def kv_half(d, array, index):
        return kv.at[array, pl.ds(pl.multiple_of(d * tok + index * hb, hb), hb), :]

    def over_x(cond, src_slot, dst_slot):
        for x_hi in range(2):
            send(
                cond, kv_half(src_slot, c, xh), kv_half(dst_slot, c, xh), net_sem.at[dst_slot, xh],
                (opp, 2 * x_hi + c),
            )

    def to_mate(cond, d, index):
        send(cond, kv_half(d, c, index), kv_half(d, c, index), mate_sem.at[d, index], mate)

    order = (xh, 1 - xh)
    for index in order:
        send(lambda: s + 2 < n_seq, kv_half(0, c, index), kv_half(2, c, index), net_sem.at[2, index], (s + 2, hd))
        if index is order[0]:
            over_x(lambda: xl == 0, 0, 1)

    def relay_two(j, parity=None):
        def here():
            return (s >= 2) if parity is None else (s >= 2) & (xl == parity)

        index = order[j]
        when_arrived(here, kv_half(2, c, index), net_sem.at[2, index])
        send(
            lambda: here() & (s + 2 < n_seq), kv_half(2, c, index), kv_half(4, c, index),
            net_sem.at[4, index], (s + 2, hd),
        )
        if j == 0:
            over_x(here, 2, 3 - 2 * xl)
        to_mate(here, 2, index)

    def relay_four(j):
        index = order[j]
        when_arrived(lambda: s >= 4, kv_half(4, c, index), net_sem.at[4, index])
        if j == 0:
            over_x(lambda: (s >= 4) & (xl == 1), 4, 3)
        to_mate(lambda: s >= 4, 4, index)

    def relay_odd(cond, d):
        for index in range(2):
            when_arrived(cond, kv_half(d, c, index), net_sem.at[d, index])
            to_mate(cond, d, index)

    def mate_ready(d):
        for index in range(2):
            arrived(kv_half(d, 1 - c, index), mate_sem.at[d, index])

    def key_range(d, qc):
        if d == 0:
            return 0, hb * (qc + 1)
        if d == REACH:
            return hb * qc, tok
        return 0, tok

    def query_range(d, kc):
        if d == 0:
            return hb * kc, tok
        if d == REACH:
            return 0, hb * (kc + 1)
        return 0, tok

    def rows_of(d, k0, k1):
        return pl.ds(pl.multiple_of(d * tok + k0, hb), k1 - k0)

    def run_hooks(h, hooks):
        for at, steps in hooks.items():
            @pl.when(h == at)
            def _(steps=steps):
                for step in steps:
                    step()

    def scores_of(d, kind, hooks):
        def body(h, carry):
            run_hooks(h, hooks)
            cols = pl.ds(pl.multiple_of(h * dh, dh), dh)
            for qc in range(2):
                k0, k1 = key_range(kind, qc)
                rows = rows_of(d, k0, k1)
                qs = slice(qc * hb, (qc + 1) * hb)
                logits = to_log2 * lax.dot_general(
                    kv[0, rows, :], q_ref[qs, cols], NT, preferred_element_type=F32
                )
                dprobs = lax.dot_general(
                    kv[1, rows, :], g_ref[qs, cols], NT, preferred_element_type=F32
                )
                if kind in (0, REACH):
                    row = lax.broadcasted_iota(jnp.int32, logits.shape, 0) + k0
                    col = lax.broadcasted_iota(jnp.int32, logits.shape, 1) + qc * hb
                    logits = jnp.where((row <= col) if kind == 0 else (row > col), logits, NEG)
                top = jnp.max(logits, axis=0, keepdims=True)
                if kind:
                    before = m_run[h, :, qs]
                    top = jnp.maximum(before, top)
                expo = jnp.exp2(logits - top)
                total = jnp.sum(expo, axis=0, keepdims=True)
                dots = jnp.sum(expo * dprobs, axis=0, keepdims=True)
                e_ref[d, h, k0:k1, qs] = expo
                ds_ref[h, rows, qs] = dprobs
                md[d, h, :, qs] = top
                if kind:
                    fade = jnp.exp2(before - top)
                    total += l_run[h, :, qs] * fade
                    dots += dl_run[h, :, qs] * fade
                m_run[h, :, qs] = top
                l_run[h, :, qs] = total
                dl_run[h, :, qs] = dots
            return carry

        lax.fori_loop(0, heads, body, 0)

    scores_of(0, 0, {})
    for d in range(1, REACH + 1):
        @pl.when(s < d)
        def _(d=d):
            kv[0, d * tok : (d + 1) * tok, :] = jnp.zeros((tok, dh), BF16)
            for h in range(heads):
                ds_ref[h, d * tok : (d + 1) * tok, :] = jnp.zeros((tok, tok), F32)

    relay_two(0)
    relay_odd(lambda: xl == 1, 1)
    odd_second = 1 + 2 * xl
    late = (xl == 0) & (s >= 4)

    @pl.when(xl == 1)
    def _():
        mate_ready(1)
        scores_of(1, 1, {2: [lambda: relay_two(1, 1)]})

    relay_two(1, 0)

    @pl.when(s >= 2)
    def _():
        mate_ready(2)
        scores_of(2, 2, {1: [lambda: relay_odd(lambda: s >= odd_second, odd_second)], 3: [lambda: relay_four(0)]})

    @pl.when(s >= odd_second)
    def _():
        mate_ready(odd_second)
        scores_of(odd_second, 1, {3: [lambda: relay_four(1)]})

    @pl.when(s >= 4)
    def _():
        mate_ready(4)
        scores_of(4, 4, {2: [lambda: relay_odd(lambda: (xl == 0) & (s >= 4), 3)]})

    @pl.when(late)
    def _():
        mate_ready(3)
        scores_of(3, 3, {})

    inverse = 1.0 / l_run[...]
    dl_run[...] = dl_run[...] * inverse
    l_run[...] = inverse

    def grads_of(d, hooks):
        into = d % 2
        acc[into] = jnp.zeros_like(acc[into])

        def body(h, carry):
            run_hooks(h, hooks)
            cols = pl.ds(pl.multiple_of(h * dh, dh), dh)
            weight = jnp.exp2(md[d, h] - m_run[h]) * l_run[h]
            delta = dl_run[h]
            for kc in range(2):
                q0, q1 = query_range(d, kc)
                ks, qs = slice(kc * hb, (kc + 1) * hb), slice(q0, q1)
                rows = slice(d * tok + kc * hb, d * tok + (kc + 1) * hb)
                probs = e_ref[d, h, ks, qs] * weight[:, q0:q1]
                dscores = probs * (ds_ref[h, rows, qs] - delta[:, q0:q1])
                probs_low, dscores_low = probs.astype(BF16), dscores.astype(BF16)
                ds_ref[h, rows, qs] = dscores
                acc[into, 1, ks, :] += lax.dot_general(
                    probs_low, g_ref[qs, cols], NN, preferred_element_type=F32
                )
                acc[into, 0, ks, :] += lax.dot_general(
                    dscores_low, q_ref[qs, cols], NN, preferred_element_type=F32
                )
            return carry

        lax.fori_loop(0, heads, body, 0)
        acc[into, 0] = acc[into, 0] * scale

    def query_grads(hooks):
        def body(h, carry):
            run_hooks(h, hooks)
            cols = pl.ds(pl.multiple_of(h * dh, dh), dh)
            for qc in range(2):
                qs = slice(qc * hb, (qc + 1) * hb)
                total = 0.0
                edge = (REACH * tok) if qc == 0 else (REACH * tok + hb)
                spans = ((0, hb), (tok, blocks * tok)) if qc == 0 else ((0, REACH * tok), (edge, blocks * tok))
                for r0, r1 in spans:
                    total += lax.dot_general(
                        ds_ref[h, r0:r1, qs].astype(BF16), kv[0, r0:r1, :], TN, preferred_element_type=F32
                    )
                dq_ref[qs, cols] = (total * scale).astype(BF16)
            return carry

        lax.fori_loop(0, heads, body, 0)

    def pair_out(d):
        @pl.when(s >= d)
        def _():
            pair_send[d] = acc[d % 2, 1 - c].astype(BF16)

        send(lambda: s >= d, pair_send.at[d], pair_recv.at[d], pair_sem.at[d], mate)

    def half_out(d):
        @pl.when(s >= d)
        def _():
            arrived(pair_recv.at[d], pair_sem.at[d])
            there, here = half(1 - xh), half(xh)
            half_send[d] = (acc[d % 2, c, there, :] + pair_recv[d, there, :].astype(F32)).astype(BF16)
            half_keep[d] = acc[d % 2, c, here, :] + pair_recv[d, here, :].astype(F32)

        send(lambda: s >= d, half_send.at[d], half_recv.at[d], half_sem.at[d], across)

    def quarter_out(d):
        @pl.when(s >= d)
        def _():
            arrived(half_recv.at[d], half_sem.at[d])
            mine = half_keep[d] + half_recv[d].astype(F32)
            if d:
                quart_send[d - 1] = mine.astype(BF16)
            else:
                own_quart[...] = mine

        if d:
            send(lambda: s >= d, quart_send.at[d - 1], quart_recv.at[d - 1], quart_sem.at[d - 1], (s - d, hd))

    plan = {
        4: {},
        3: {2: [lambda: half_out(4)]},
        2: {2: [lambda: half_out(3)]},
        1: {2: [lambda: half_out(2), lambda: quarter_out(4)]},
        0: {2: [lambda: half_out(1), lambda: quarter_out(3)]},
    }
    for d in range(REACH, -1, -1):
        @pl.when(s >= d)
        def _(d=d):
            grads_of(d, plan[d])

        pair_out(d)
    query_grads({1: [lambda: half_out(0)], 2: [lambda: quarter_out(2)]})
    write_dq = pltpu.make_async_copy(dq_ref, dq_out, load_sem.at[0])
    write_dq.start()
    quarter_out(1)
    quarter_out(0)
    for d in range(REACH, 0, -1):
        @pl.when(s + d < n_seq)
        def _(d=d):
            arrived(quart_recv.at[d - 1], quart_sem.at[d - 1])
            own_quart[...] += quart_recv[d - 1].astype(F32)

    def fin_half(array, index):
        return fin.at[array, half(index), :]

    fin[c, half(xh), :] = own_quart[...].astype(BF16)
    always = lambda: s >= 0
    send(always, fin_half(c, xh), fin_half(c, xh), fin_sem.at[0], across)
    send(always, fin_half(c, xh), fin_half(c, xh), fin_sem.at[1], mate)
    arrived(fin_half(c, 1 - xh), fin_sem.at[0])
    send(always, fin_half(c, 1 - xh), fin_half(c, 1 - xh), fin_sem.at[2], mate)
    arrived(fin_half(1 - c, xh), fin_sem.at[1])
    arrived(fin_half(1 - c, 1 - xh), fin_sem.at[2])
    fin_out[...] = fin[...]
    write_dq.wait()
    wait_sent()


def on_device(query, key_rows, value_rows, grad_out):
    tok, dh = key_rows.shape
    heads = query.shape[1] // dh
    blocks = REACH + 1
    vmem = pltpu.VMEM
    dma = pltpu.SemaphoreType.DMA
    grad_query, fin = pl.pallas_call(
        kernel,
        out_shape=(
            jax.ShapeDtypeStruct(query.shape, BF16),
            jax.ShapeDtypeStruct((2, tok, dh), BF16),
        ),
        in_specs=[pl.BlockSpec(memory_space=pl.ANY)] * 4,
        out_specs=(pl.BlockSpec(memory_space=pl.ANY), pl.BlockSpec(memory_space=vmem)),
        scratch_shapes=[
            vmem((tok, heads * dh), BF16),
            vmem((tok, heads * dh), BF16),
            vmem((2, blocks * tok, dh), BF16),
            vmem((blocks, heads, tok, tok), F32),
            vmem((heads, blocks * tok, tok), F32),
            vmem((blocks, heads, 1, tok), F32),
            vmem((heads, 1, tok), F32),
            vmem((heads, 1, tok), F32),
            vmem((heads, 1, tok), F32),
            vmem((tok, heads * dh), BF16),
            vmem((2, 2, tok, dh), F32),
            vmem((blocks, tok, dh), BF16),
            vmem((blocks, tok, dh), BF16),
            vmem((blocks, tok // 2, dh), F32),
            vmem((blocks, tok // 2, dh), BF16),
            vmem((blocks, tok // 2, dh), BF16),
            vmem((REACH, tok // 2, dh), BF16),
            vmem((REACH, tok // 2, dh), BF16),
            vmem((tok // 2, dh), F32),
            vmem((2, tok, dh), BF16),
            dma((4,)),
            dma((64,)),
            dma((blocks, 2)),
            dma((blocks, 2)),
            dma((blocks,)),
            dma((blocks,)),
            dma((REACH,)),
            dma((3,)),
        ],
        compiler_params=pltpu.CompilerParams(
            collective_id=0, has_side_effects=True, vmem_limit_bytes=67043328
        ),
    )(query, grad_out, key_rows, value_rows)
    return grad_query, fin[0].astype(F32), fin[1].astype(F32)


def solution(mesh):
    return jax.shard_map(
        on_device,
        mesh=mesh,
        in_specs=(P("seq", "head"), P("seq", None), P("seq", None), P("seq", "head")),
        out_specs=(P("seq", "head"), P("seq", None), P("seq", None)),
        check_vma=False,
    )
```

```python
import jax
import jax.numpy as jnp
from jax import lax
from jax.experimental import pallas as pl
from jax.experimental.pallas import tpu as pltpu
from jax.sharding import PartitionSpec as P

F32 = jnp.float32
BF16 = jnp.bfloat16
MESH = pl.DeviceIdType.MESH
REACH = 4
LOG2E = 1.4426950408889634
NEG = -1e30
NT = (((1,), (1,)), ((), ()))
NN = (((1,), (0,)), ((), ()))
TN = (((0,), (0,)), ((), ()))


def kernel(
    q_hbm, g_hbm, k_hbm, v_hbm,
    dq_out, fin_out,
    q_ref, g_ref, kv, e_ref, ds_ref, md, m_run, l_run, dl_run, dq_ref,
    acc, pair_send, pair_recv, half_keep, half_send, half_recv,
    quart_send, quart_recv, own_quart, fin,
    load_sem, send_sem, net_sem, mate_sem, pair_sem, half_sem, quart_sem, fin_sem,
):
    tok, dh = e_ref.shape[2], kv.shape[2]
    heads = e_ref.shape[1]
    hb = tok // 2
    blocks = REACH + 1
    scale = dh ** (-0.5)
    to_log2 = scale * LOG2E
    n_seq = lax.axis_size("seq")
    s, hd = lax.axis_index("seq"), lax.axis_index("head")
    xl, xh, c = lax.rem(s, 2), lax.div(hd, 2), lax.rem(hd, 2)
    opp = s + 1 - 2 * xl
    mate = (s, hd + 1 - 2 * c)
    across = (s, lax.rem(hd + 2, 4))

    def half(index):
        return pl.ds(pl.multiple_of(index * hb, hb), hb)

    loads = [
        pltpu.make_async_copy(src, dst, load_sem.at[i])
        for i, (src, dst) in enumerate(
            ((k_hbm, kv.at[0, :tok]), (v_hbm, kv.at[1, :tok]), (q_hbm, q_ref), (g_hbm, g_ref))
        )
    ]
    for load in loads:
        load.start()
    barrier = pltpu.get_barrier_semaphore()

    def greet(device):
        pl.semaphore_signal(barrier, inc=1, device_id=device, device_id_type=MESH)

    for head in (hd, across[1]):
        greet((opp, head))
    greet(mate)
    greet(across)
    for d in range(1, REACH + 1):
        @pl.when(s + d < n_seq)
        def _(d=d):
            greet((s + d, hd))

        @pl.when(s >= d)
        def _(d=d):
            greet((s - d, hd))
    ahead = jnp.minimum(n_seq - 1 - s, REACH)
    behind = jnp.minimum(s, REACH)
    pl.semaphore_wait(barrier, 4 + ahead + behind)
    for load in loads[:2]:
        load.wait()

    pending = []

    def send(cond, src, dst, recv_sem, device):
        sem = send_sem.at[len(pending)]
        pending.append((cond, src.shape[0]))

        @pl.when(cond())
        def _():
            pltpu.make_async_remote_copy(
                src_ref=src, dst_ref=dst, send_sem=sem, recv_sem=recv_sem,
                device_id=device, device_id_type=MESH,
            ).start()

    def wait_sent():
        for i, (cond, size) in enumerate(pending):
            @pl.when(cond())
            def _(i=i, size=size):
                buf = pair_send.at[0, :size]
                pltpu.make_async_remote_copy(
                    src_ref=buf, dst_ref=buf, send_sem=send_sem.at[i], recv_sem=fin_sem.at[0],
                    device_id=mate, device_id_type=MESH,
                ).wait_send()

    def arrived(buf, sem):
        pltpu.make_async_remote_copy(
            src_ref=buf, dst_ref=buf, send_sem=send_sem.at[0], recv_sem=sem,
            device_id=mate, device_id_type=MESH,
        ).wait_recv()

    def when_arrived(cond, buf, sem):
        @pl.when(cond())
        def _():
            arrived(buf, sem)

    def kv_half(d, array, index):
        return kv.at[array, pl.ds(pl.multiple_of(d * tok + index * hb, hb), hb), :]

    def over_x(cond, src_slot, dst_slot):
        for x_hi in range(2):
            send(
                cond, kv_half(src_slot, c, xh), kv_half(dst_slot, c, xh), net_sem.at[dst_slot, xh],
                (opp, 2 * x_hi + c),
            )

    def to_mate(cond, d, index):
        send(cond, kv_half(d, c, index), kv_half(d, c, index), mate_sem.at[d, index], mate)

    order = (xh, 1 - xh)
    for index in order:
        send(lambda: s + 2 < n_seq, kv_half(0, c, index), kv_half(2, c, index), net_sem.at[2, index], (s + 2, hd))
        if index is order[0]:
            over_x(lambda: xl == 0, 0, 1)

    def relay_two(j, parity=None):
        def here():
            return (s >= 2) if parity is None else (s >= 2) & (xl == parity)

        index = order[j]
        when_arrived(here, kv_half(2, c, index), net_sem.at[2, index])
        send(
            lambda: here() & (s + 2 < n_seq), kv_half(2, c, index), kv_half(4, c, index),
            net_sem.at[4, index], (s + 2, hd),
        )
        if j == 0:
            over_x(here, 2, 3 - 2 * xl)
        to_mate(here, 2, index)

    def relay_four(j):
        index = order[j]
        when_arrived(lambda: s >= 4, kv_half(4, c, index), net_sem.at[4, index])
        if j == 0:
            over_x(lambda: (s >= 4) & (xl == 1), 4, 3)
        to_mate(lambda: s >= 4, 4, index)

    def relay_odd(cond, d):
        for index in range(2):
            when_arrived(cond, kv_half(d, c, index), net_sem.at[d, index])
            to_mate(cond, d, index)

    def mate_ready(d):
        for index in range(2):
            arrived(kv_half(d, 1 - c, index), mate_sem.at[d, index])

    def key_range(d, qc):
        if d == 0:
            return 0, hb * (qc + 1)
        if d == REACH:
            return hb * qc, tok
        return 0, tok

    def query_range(d, kc):
        if d == 0:
            return hb * kc, tok
        if d == REACH:
            return 0, hb * (kc + 1)
        return 0, tok

    def rows_of(d, k0, k1):
        return pl.ds(pl.multiple_of(d * tok + k0, hb), k1 - k0)

    def run_hooks(h, hooks):
        for at, steps in hooks.items():
            @pl.when(h == at)
            def _(steps=steps):
                for step in steps:
                    step()

    def scores_of(d, kind):
        for h in range(heads):
            cols = slice(h * dh, (h + 1) * dh)
            for qc in range(2):
                k0, k1 = key_range(kind, qc)
                rows = rows_of(d, k0, k1)
                qs = slice(qc * hb, (qc + 1) * hb)
                logits = to_log2 * lax.dot_general(
                    kv[0, rows, :], q_ref[qs, cols], NT, preferred_element_type=F32
                )
                dprobs = lax.dot_general(
                    kv[1, rows, :], g_ref[qs, cols], NT, preferred_element_type=F32
                )
                if kind in (0, REACH):
                    row = lax.broadcasted_iota(jnp.int32, logits.shape, 0) + k0
                    col = lax.broadcasted_iota(jnp.int32, logits.shape, 1) + qc * hb
                    logits = jnp.where((row <= col) if kind == 0 else (row > col), logits, NEG)
                top = jnp.max(logits, axis=0, keepdims=True)
                if kind:
                    before = m_run[h, :, qs]
                    top = jnp.maximum(before, top)
                expo = jnp.exp2(logits - top)
                total = jnp.sum(expo, axis=0, keepdims=True)
                dots = jnp.sum(expo * dprobs, axis=0, keepdims=True)
                e_ref[d, h, k0:k1, qs] = expo
                ds_ref[h, rows, qs] = dprobs
                md[d, h, :, qs] = top
                if kind:
                    fade = jnp.exp2(before - top)
                    total += l_run[h, :, qs] * fade
                    dots += dl_run[h, :, qs] * fade
                m_run[h, :, qs] = top
                l_run[h, :, qs] = total
                dl_run[h, :, qs] = dots

    for load in loads[2:]:
        load.wait()
    scores_of(0, 0)
    for d in range(1, REACH + 1):
        @pl.when(s < d)
        def _(d=d):
            kv[0, d * tok : (d + 1) * tok, :] = jnp.zeros((tok, dh), BF16)
            for h in range(heads):
                ds_ref[h, d * tok : (d + 1) * tok, :] = jnp.zeros((tok, tok), F32)

    relay_two(0)
    relay_two(1, 0)
    relay_odd(lambda: xl == 1, 1)
    first, second = 2 - xl, 1 + xl

    @pl.when(s >= first)
    def _():
        mate_ready(first)
        scores_of(first, 1)

    relay_two(1, 1)
    relay_odd(lambda: (xl == 0) & (s >= 1), 1)
    relay_four(0)

    @pl.when(s >= second)
    def _():
        mate_ready(second)
        scores_of(second, 1)

    relay_odd(lambda: (xl == 1) & (s >= 3), 3)
    relay_four(1)

    @pl.when(s >= 4)
    def _():
        mate_ready(4)
        scores_of(4, 4)

    relay_odd(lambda: (xl == 0) & (s >= 3), 3)

    @pl.when(s >= 3)
    def _():
        mate_ready(3)
        scores_of(3, 3)

    inverse = 1.0 / l_run[...]
    dl_run[...] = dl_run[...] * inverse
    l_run[...] = inverse

    def grads_of(d):
        into = d % 2
        for kc in range(2):
            q0, q1 = query_range(d, kc)
            ks, qs = slice(kc * hb, (kc + 1) * hb), slice(q0, q1)
            rows = slice(d * tok + kc * hb, d * tok + (kc + 1) * hb)
            for h in range(heads):
                cols = slice(h * dh, (h + 1) * dh)
                weight = jnp.exp2(md[d, h, :, qs] - m_run[h, :, qs]) * l_run[h, :, qs]
                probs = e_ref[d, h, ks, qs] * weight
                dscores = probs * (ds_ref[h, rows, qs] - dl_run[h, :, qs])
                ds_ref[h, rows, qs] = dscores
                to_value = lax.dot_general(
                    probs.astype(BF16), g_ref[qs, cols], NN, preferred_element_type=F32
                )
                to_key = lax.dot_general(
                    dscores.astype(BF16), q_ref[qs, cols], NN, preferred_element_type=F32
                )
                if h:
                    to_value += acc[into, 1, ks, :]
                    to_key += acc[into, 0, ks, :]
                acc[into, 1, ks, :] = to_value
                acc[into, 0, ks, :] = to_key * scale if h == heads - 1 else to_key

    def query_grads(hooks):
        def body(h, carry):
            run_hooks(h, hooks)
            cols = pl.ds(pl.multiple_of(h * dh, dh), dh)
            for qc in range(2):
                qs = slice(qc * hb, (qc + 1) * hb)
                total = 0.0
                edge = (REACH * tok) if qc == 0 else (REACH * tok + hb)
                spans = ((0, hb), (tok, blocks * tok)) if qc == 0 else ((0, REACH * tok), (edge, blocks * tok))
                for r0, r1 in spans:
                    total += lax.dot_general(
                        ds_ref[h, r0:r1, qs].astype(BF16), kv[0, r0:r1, :], TN, preferred_element_type=F32
                    )
                dq_ref[qs, cols] = (total * scale).astype(BF16)
            return carry

        lax.fori_loop(0, heads, body, 0)

    def pair_out(d):
        @pl.when(s >= d)
        def _():
            pair_send[d] = acc[d % 2, 1 - c].astype(BF16)

        send(lambda: s >= d, pair_send.at[d], pair_recv.at[d], pair_sem.at[d], mate)

    def half_out(d):
        @pl.when(s >= d)
        def _():
            arrived(pair_recv.at[d], pair_sem.at[d])
            there, here = half(1 - xh), half(xh)
            half_send[d] = (acc[d % 2, c, there, :] + pair_recv[d, there, :].astype(F32)).astype(BF16)
            half_keep[d] = acc[d % 2, c, here, :] + pair_recv[d, here, :].astype(F32)

        send(lambda: s >= d, half_send.at[d], half_recv.at[d], half_sem.at[d], across)

    def quarter_out(d):
        @pl.when(s >= d)
        def _():
            arrived(half_recv.at[d], half_sem.at[d])
            mine = half_keep[d] + half_recv[d].astype(F32)
            if d:
                quart_send[d - 1] = mine.astype(BF16)
            else:
                own_quart[...] = mine

        if d:
            send(lambda: s >= d, quart_send.at[d - 1], quart_recv.at[d - 1], quart_sem.at[d - 1], (s - d, hd))

    for d in range(REACH, -1, -1):
        @pl.when(s >= d)
        def _(d=d):
            grads_of(d)

        pair_out(d)
        if d < REACH:
            half_out(d + 1)
    half_out(0)
    query_grads({0: [lambda: quarter_out(4)], 1: [lambda: quarter_out(3)], 3: [lambda: quarter_out(2)]})
    write_dq = pltpu.make_async_copy(dq_ref, dq_out, load_sem.at[0])
    write_dq.start()
    quarter_out(1)
    quarter_out(0)
    for d in range(REACH, 0, -1):
        @pl.when(s + d < n_seq)
        def _(d=d):
            arrived(quart_recv.at[d - 1], quart_sem.at[d - 1])
            own_quart[...] += quart_recv[d - 1].astype(F32)

    def fin_half(array, index):
        return fin.at[array, half(index), :]

    fin[c, half(xh), :] = own_quart[...].astype(BF16)
    always = lambda: s >= 0
    send(always, fin_half(c, xh), fin_half(c, xh), fin_sem.at[0], across)
    send(always, fin_half(c, xh), fin_half(c, xh), fin_sem.at[1], mate)
    arrived(fin_half(c, 1 - xh), fin_sem.at[0])
    send(always, fin_half(c, 1 - xh), fin_half(c, 1 - xh), fin_sem.at[2], mate)
    arrived(fin_half(1 - c, xh), fin_sem.at[1])
    arrived(fin_half(1 - c, 1 - xh), fin_sem.at[2])
    write_fin = pltpu.make_async_copy(fin, fin_out, load_sem.at[1])
    write_fin.start()
    write_fin.wait()
    write_dq.wait()
    wait_sent()


def finish(dq_hbm, fin_hbm, dq_out, dk_out, dv_out, dq_buf, fin_buf, wide, in_sem, out_sem):
    parts = dq_buf.shape[0]
    rows = dq_buf.shape[1]
    fin_in = pltpu.make_async_copy(fin_hbm, fin_buf, in_sem.at[parts])
    fin_in.start()

    def span(i):
        return slice(i * rows, (i + 1) * rows)

    loads = [pltpu.make_async_copy(dq_hbm.at[span(i)], dq_buf.at[i], in_sem.at[i]) for i in range(parts)]
    stores = [pltpu.make_async_copy(dq_buf.at[i], dq_out.at[span(i)], out_sem.at[i]) for i in range(parts)]
    for load in loads:
        load.start()
    fin_in.wait()
    for array, out in enumerate((dk_out, dv_out)):
        wide[array] = fin_buf[array].astype(F32)
        stores.append(pltpu.make_async_copy(wide.at[array], out, out_sem.at[parts + array]))
        stores[-1].start()
    for load, store in zip(loads, stores):
        load.wait()
        store.start()
    for store in stores:
        store.wait()


def on_device(query, key_rows, value_rows, grad_out):
    tok, dh = key_rows.shape
    heads = query.shape[1] // dh
    blocks = REACH + 1
    vmem = pltpu.VMEM
    dma = pltpu.SemaphoreType.DMA
    grad_query, fin = pl.pallas_call(
        kernel,
        out_shape=(
            jax.ShapeDtypeStruct(query.shape, BF16),
            jax.ShapeDtypeStruct((2, tok, dh), BF16),
        ),
        in_specs=[pl.BlockSpec(memory_space=pl.ANY)] * 4,
        out_specs=(pl.BlockSpec(memory_space=pl.ANY),) * 2,
        scratch_shapes=[
            vmem((tok, heads * dh), BF16),
            vmem((tok, heads * dh), BF16),
            vmem((2, blocks * tok, dh), BF16),
            vmem((blocks, heads, tok, tok), F32),
            vmem((heads, blocks * tok, tok), F32),
            vmem((blocks, heads, 1, tok), F32),
            vmem((heads, 1, tok), F32),
            vmem((heads, 1, tok), F32),
            vmem((heads, 1, tok), F32),
            vmem((tok, heads * dh), BF16),
            vmem((2, 2, tok, dh), F32),
            vmem((blocks, tok, dh), BF16),
            vmem((blocks, tok, dh), BF16),
            vmem((blocks, tok // 2, dh), F32),
            vmem((blocks, tok // 2, dh), BF16),
            vmem((blocks, tok // 2, dh), BF16),
            vmem((REACH, tok // 2, dh), BF16),
            vmem((REACH, tok // 2, dh), BF16),
            vmem((tok // 2, dh), F32),
            vmem((2, tok, dh), BF16),
            dma((4,)),
            dma((64,)),
            dma((blocks, 2)),
            dma((blocks, 2)),
            dma((blocks,)),
            dma((blocks,)),
            dma((REACH,)),
            dma((3,)),
        ],
        compiler_params=pltpu.CompilerParams(
            collective_id=0, has_side_effects=True, vmem_limit_bytes=67043328
        ),
    )(query, grad_out, key_rows, value_rows)
    parts = 4
    anywhere = pl.BlockSpec(memory_space=pl.ANY)
    return pl.pallas_call(
        finish,
        out_shape=(
            jax.ShapeDtypeStruct(query.shape, BF16),
            jax.ShapeDtypeStruct((tok, dh), F32),
            jax.ShapeDtypeStruct((tok, dh), F32),
        ),
        in_specs=[anywhere] * 2,
        out_specs=(anywhere,) * 3,
        scratch_shapes=[
            vmem((parts, tok // parts, heads * dh), BF16),
            vmem((2, tok, dh), BF16),
            vmem((2, tok, dh), F32),
            dma((parts + 1,)),
            dma((parts + 2,)),
        ],
    )(grad_query, fin)


def solution(mesh):
    return jax.shard_map(
        on_device,
        mesh=mesh,
        in_specs=(P("seq", "head"), P("seq", None), P("seq", None), P("seq", "head")),
        out_specs=(P("seq", "head"), P("seq", None), P("seq", None)),
        check_vma=False,
    )
```

```python
import jax
import jax.numpy as jnp
from jax import lax
from jax.experimental import pallas as pl
from jax.experimental.pallas import tpu as pltpu
from jax.sharding import PartitionSpec as P

F32 = jnp.float32
BF16 = jnp.bfloat16
MESH = pl.DeviceIdType.MESH
REACH = 4
LOG2E = 1.4426950408889634
NEG = -1e30
NT = (((1,), (1,)), ((), ()))
NN = (((1,), (0,)), ((), ()))
TN = (((0,), (0,)), ((), ()))


def kernel(
    q_hbm, g_hbm, k_hbm, v_hbm,
    dq_out, fin_out,
    q_ref, g_ref, kv, e_ref, ds_ref, md, m_run, l_run, dl_run, dq_ref,
    acc, pair_send, pair_recv, keep, odd_send, opp_recv, chain_send, chain_recv,
    fin_send, fin_recv, fin,
    load_sem, send_sem, net_sem, mate_sem, pair_sem, opp_sem, chain_sem, across_sem, fin_sem,
):
    tok, dh = e_ref.shape[2], kv.shape[2]
    heads = e_ref.shape[1]
    hb = tok // 2
    blocks = REACH + 1
    scale = dh ** (-0.5)
    to_log2 = scale * LOG2E
    n_seq = lax.axis_size("seq")
    s, hd = lax.axis_index("seq"), lax.axis_index("head")
    xl, xh, c = lax.rem(s, 2), lax.div(hd, 2), lax.rem(hd, 2)
    opp = s + 1 - 2 * xl
    mate = (s, hd + 1 - 2 * c)
    across = (s, lax.rem(hd + 2, 4))

    def half(index):
        return pl.ds(pl.multiple_of(index * hb, hb), hb)

    loads = [
        pltpu.make_async_copy(src, dst, load_sem.at[i])
        for i, (src, dst) in enumerate(
            ((k_hbm, kv.at[0, :tok]), (v_hbm, kv.at[1, :tok]), (q_hbm, q_ref), (g_hbm, g_ref))
        )
    ]
    for load in loads:
        load.start()
    barrier = pltpu.get_barrier_semaphore()

    def greet(device):
        pl.semaphore_signal(barrier, inc=1, device_id=device, device_id_type=MESH)

    for head in (hd, across[1]):
        greet((opp, head))
    greet(mate)
    greet(across)

    @pl.when(s + 2 < n_seq)
    def _():
        greet((s + 2, hd))

    @pl.when(s >= 2)
    def _():
        greet((s - 2, hd))

    pl.semaphore_wait(barrier, 4 + jnp.minimum(n_seq - 1 - s, 2) // 2 + jnp.minimum(s, 2) // 2)
    for load in loads[:2]:
        load.wait()

    pending = []

    def send(cond, src, dst, recv_sem, device):
        sem = send_sem.at[len(pending)]
        pending.append((cond, src.shape[0]))

        @pl.when(cond())
        def _():
            pltpu.make_async_remote_copy(
                src_ref=src, dst_ref=dst, send_sem=sem, recv_sem=recv_sem,
                device_id=device, device_id_type=MESH,
            ).start()

    def wait_sent():
        for i, (cond, size) in enumerate(pending):
            @pl.when(cond())
            def _(i=i, size=size):
                buf = pair_send.at[0, :size]
                pltpu.make_async_remote_copy(
                    src_ref=buf, dst_ref=buf, send_sem=send_sem.at[i], recv_sem=fin_sem.at[0],
                    device_id=mate, device_id_type=MESH,
                ).wait_send()

    def arrived(buf, sem):
        pltpu.make_async_remote_copy(
            src_ref=buf, dst_ref=buf, send_sem=send_sem.at[0], recv_sem=sem,
            device_id=mate, device_id_type=MESH,
        ).wait_recv()

    def when_arrived(cond, buf, sem):
        @pl.when(cond())
        def _():
            arrived(buf, sem)

    def kv_half(d, array, index):
        return kv.at[array, pl.ds(pl.multiple_of(d * tok + index * hb, hb), hb), :]

    def over_x(cond, src_slot, dst_slot):
        for x_hi in range(2):
            send(
                cond, kv_half(src_slot, c, xh), kv_half(dst_slot, c, xh), net_sem.at[dst_slot, xh],
                (opp, 2 * x_hi + c),
            )

    def to_mate(cond, d, index):
        send(cond, kv_half(d, c, index), kv_half(d, c, index), mate_sem.at[d, index], mate)

    order = (xh, 1 - xh)
    for index in order:
        send(lambda: s + 2 < n_seq, kv_half(0, c, index), kv_half(2, c, index), net_sem.at[2, index], (s + 2, hd))
        if index is order[0]:
            over_x(lambda: xl == 0, 0, 1)

    def relay_two(j, parity=None):
        def here():
            return (s >= 2) if parity is None else (s >= 2) & (xl == parity)

        index = order[j]
        when_arrived(here, kv_half(2, c, index), net_sem.at[2, index])
        send(
            lambda: here() & (s + 2 < n_seq), kv_half(2, c, index), kv_half(4, c, index),
            net_sem.at[4, index], (s + 2, hd),
        )
        if j == 0:
            over_x(here, 2, 3 - 2 * xl)
        to_mate(here, 2, index)

    def relay_four(j):
        index = order[j]
        when_arrived(lambda: s >= 4, kv_half(4, c, index), net_sem.at[4, index])
        if j == 0:
            over_x(lambda: (s >= 4) & (xl == 1), 4, 3)
        to_mate(lambda: s >= 4, 4, index)

    def relay_odd(cond, d):
        for index in range(2):
            when_arrived(cond, kv_half(d, c, index), net_sem.at[d, index])
            to_mate(cond, d, index)

    def mate_ready(d):
        for index in range(2):
            arrived(kv_half(d, 1 - c, index), mate_sem.at[d, index])

    def key_range(d, qc):
        if d == 0:
            return 0, hb * (qc + 1)
        if d == REACH:
            return hb * qc, tok
        return 0, tok

    def query_range(d, kc):
        if d == 0:
            return hb * kc, tok
        if d == REACH:
            return 0, hb * (kc + 1)
        return 0, tok

    def rows_of(d, k0, k1):
        return pl.ds(pl.multiple_of(d * tok + k0, hb), k1 - k0)

    def run_hooks(h, hooks):
        for at, steps in hooks.items():
            @pl.when(h == at)
            def _(steps=steps):
                for step in steps:
                    step()

    def scores_of(d, kind):
        for h in range(heads):
            cols = slice(h * dh, (h + 1) * dh)
            for qc in range(2):
                k0, k1 = key_range(kind, qc)
                rows = rows_of(d, k0, k1)
                qs = slice(qc * hb, (qc + 1) * hb)
                logits = to_log2 * lax.dot_general(
                    kv[0, rows, :], q_ref[qs, cols], NT, preferred_element_type=F32
                )
                dprobs = lax.dot_general(
                    kv[1, rows, :], g_ref[qs, cols], NT, preferred_element_type=F32
                )
                if kind in (0, REACH):
                    row = lax.broadcasted_iota(jnp.int32, logits.shape, 0) + k0
                    col = lax.broadcasted_iota(jnp.int32, logits.shape, 1) + qc * hb
                    logits = jnp.where((row <= col) if kind == 0 else (row > col), logits, NEG)
                top = jnp.max(logits, axis=0, keepdims=True)
                if kind:
                    before = m_run[h, :, qs]
                    top = jnp.maximum(before, top)
                expo = jnp.exp2(logits - top)
                total = jnp.sum(expo, axis=0, keepdims=True)
                dots = jnp.sum(expo * dprobs, axis=0, keepdims=True)
                e_ref[d, h, k0:k1, qs] = expo
                ds_ref[h, rows, qs] = dprobs
                md[d, h, :, qs] = top
                if kind:
                    fade = jnp.exp2(before - top)
                    total += l_run[h, :, qs] * fade
                    dots += dl_run[h, :, qs] * fade
                m_run[h, :, qs] = top
                l_run[h, :, qs] = total
                dl_run[h, :, qs] = dots

    for load in loads[2:]:
        load.wait()
    scores_of(0, 0)
    for d in range(1, REACH + 1):
        @pl.when(s < d)
        def _(d=d):
            kv[0, d * tok : (d + 1) * tok, :] = jnp.zeros((tok, dh), BF16)
            for h in range(heads):
                ds_ref[h, d * tok : (d + 1) * tok, :] = jnp.zeros((tok, tok), F32)

    relay_two(0)
    relay_two(1, 0)
    relay_odd(lambda: xl == 1, 1)
    first, second = 2 - xl, 1 + xl

    @pl.when(s >= first)
    def _():
        mate_ready(first)
        scores_of(first, 1)

    relay_two(1, 1)
    relay_odd(lambda: (xl == 0) & (s >= 1), 1)
    relay_four(0)

    @pl.when(s >= second)
    def _():
        mate_ready(second)
        scores_of(second, 1)

    relay_odd(lambda: (xl == 1) & (s >= 3), 3)
    relay_four(1)

    @pl.when(s >= 4)
    def _():
        mate_ready(4)
        scores_of(4, 4)

    relay_odd(lambda: (xl == 0) & (s >= 3), 3)

    @pl.when(s >= 3)
    def _():
        mate_ready(3)
        scores_of(3, 3)

    inverse = 1.0 / l_run[...]
    dl_run[...] = dl_run[...] * inverse
    l_run[...] = inverse

    def grads_of(d, into):
        for kc in range(2):
            q0, q1 = query_range(d, kc)
            ks, qs = slice(kc * hb, (kc + 1) * hb), slice(q0, q1)
            rows = slice(d * tok + kc * hb, d * tok + (kc + 1) * hb)
            for h in range(heads):
                cols = slice(h * dh, (h + 1) * dh)
                weight = jnp.exp2(md[d, h, :, qs] - m_run[h, :, qs]) * l_run[h, :, qs]
                probs = e_ref[d, h, ks, qs] * weight
                dscores = probs * (ds_ref[h, rows, qs] - dl_run[h, :, qs])
                ds_ref[h, rows, qs] = dscores
                to_value = lax.dot_general(
                    probs.astype(BF16), g_ref[qs, cols], NN, preferred_element_type=F32
                )
                to_key = lax.dot_general(
                    dscores.astype(BF16), q_ref[qs, cols], NN, preferred_element_type=F32
                )
                if h:
                    to_value += acc[into, 1, ks, :]
                    to_key += acc[into, 0, ks, :]
                acc[into, 1, ks, :] = to_value
                acc[into, 0, ks, :] = to_key * scale if h == heads - 1 else to_key

    def query_grads(hooks):
        def body(h, carry):
            run_hooks(h, hooks)
            cols = pl.ds(pl.multiple_of(h * dh, dh), dh)
            for qc in range(2):
                qs = slice(qc * hb, (qc + 1) * hb)
                total = 0.0
                edge = (REACH * tok) if qc == 0 else (REACH * tok + hb)
                spans = ((0, hb), (tok, blocks * tok)) if qc == 0 else ((0, REACH * tok), (edge, blocks * tok))
                for r0, r1 in spans:
                    total += lax.dot_general(
                        ds_ref[h, r0:r1, qs].astype(BF16), kv[0, r0:r1, :], TN, preferred_element_type=F32
                    )
                dq_ref[qs, cols] = (total * scale).astype(BF16)
            return carry

        lax.fori_loop(0, heads, body, 0)

    def pair_out(d):
        @pl.when(s >= d)
        def _():
            pair_send[d] = acc[place[d], 1 - c].astype(BF16)

        send(lambda: s >= d, pair_send.at[d], pair_recv.at[d], pair_sem.at[d], mate)

    def odd_out(d):
        o = d // 2

        @pl.when(s >= d)
        def _():
            arrived(pair_recv.at[d], pair_sem.at[d])
            odd_send[o] = (acc[place[d], c] + pair_recv[d].astype(F32)).astype(BF16)

        for x_hi in range(2):
            send(
                lambda: s >= d, odd_send.at[o, x_hi * hb : (x_hi + 1) * hb], opp_recv.at[o, xh],
                opp_sem.at[o, xh], (opp, 2 * x_hi + c),
            )

    def base(d):
        @pl.when(s >= d)
        def _():
            arrived(pair_recv.at[d], pair_sem.at[d])
            keep[d // 2] = acc[place[d], c] + pair_recv[d].astype(F32)

    def add_opp(o):
        @pl.when(s >= 2 * o + 2 * xl)
        def _():
            for x_hi in range(2):
                arrived(opp_recv.at[o, x_hi], opp_sem.at[o, x_hi])
            keep[o + xl, half(xh), :] += opp_recv[o, 0].astype(F32) + opp_recv[o, 1].astype(F32)

    def add_chain(i, index):
        @pl.when((s >= 2 - 2 * i) & (s + 2 < n_seq))
        def _():
            arrived(chain_recv.at[i, half(index), :], chain_sem.at[i, index])
            keep[1 - i, half(index), :] += chain_recv[i, half(index), :].astype(F32)

    def chain_out(i, index, parity=None):
        def here():
            some = s >= 4 - 2 * i
            return some if parity is None else some & (xl == parity)

        @pl.when(here())
        def _():
            chain_send[i, half(index), :] = keep[2 - i, half(index), :].astype(BF16)

        send(
            here, chain_send.at[i, half(index), :], chain_recv.at[i, half(index), :],
            chain_sem.at[i, index], (s - 2, hd),
        )

    def first_chain():
        base(4)
        chain_out(0, 1 - xh)
        chain_out(0, xh, 0)

    def second_base():
        base(2)

    def last_of_four():
        add_opp(1)
        chain_out(0, xh, 1)

    def early_two():
        add_chain(0, 1 - xh)
        chain_out(1, 1 - xh)

    steps = ((3, None), (4, lambda: odd_out(3)), (1, first_chain), (2, lambda: odd_out(1)), (0, second_base))
    place = {d: i % 2 for i, (d, _) in enumerate(steps)}
    for d, after in steps:
        @pl.when(s >= d)
        def _(d=d):
            grads_of(d, place[d])

        pair_out(d)
        if after is not None:
            after()
    query_grads({0: [last_of_four], 1: [lambda: base(0)], 2: [early_two]})
    write_dq = pltpu.make_async_copy(dq_ref, dq_out, load_sem.at[0])
    write_dq.start()
    add_opp(0)
    add_chain(0, xh)
    chain_out(1, xh)
    always = lambda: s >= 0
    for index in (1 - xh, xh):
        rows = half(index)
        add_chain(1, index)
        fin_send[rows, :] = keep[0, rows, :].astype(BF16)
        send(always, fin_send.at[rows, :], fin_recv.at[rows, :], across_sem.at[index], across)
    for index in (xh, 1 - xh):
        rows = half(index)
        arrived(fin_recv.at[rows, :], across_sem.at[index])
        fin[c, rows, :] = (fin_send[rows, :].astype(F32) + fin_recv[rows, :].astype(F32)).astype(BF16)
        send(always, fin.at[c, rows, :], fin.at[c, rows, :], fin_sem.at[index], mate)
    for index in (xh, 1 - xh):
        arrived(fin.at[1 - c, half(index), :], fin_sem.at[index])
    write_fin = pltpu.make_async_copy(fin, fin_out, load_sem.at[1])
    write_fin.start()
    write_fin.wait()
    write_dq.wait()
    wait_sent()


def finish(dq_hbm, fin_hbm, dq_out, dk_out, dv_out, dq_buf, fin_buf, wide, in_sem, out_sem):
    parts = dq_buf.shape[0]
    rows = dq_buf.shape[1]
    fin_in = pltpu.make_async_copy(fin_hbm, fin_buf, in_sem.at[parts])
    fin_in.start()

    def span(i):
        return slice(i * rows, (i + 1) * rows)

    loads = [pltpu.make_async_copy(dq_hbm.at[span(i)], dq_buf.at[i], in_sem.at[i]) for i in range(parts)]
    stores = [pltpu.make_async_copy(dq_buf.at[i], dq_out.at[span(i)], out_sem.at[i]) for i in range(parts)]
    for load in loads:
        load.start()
    fin_in.wait()
    for array, out in enumerate((dk_out, dv_out)):
        wide[array] = fin_buf[array].astype(F32)
        stores.append(pltpu.make_async_copy(wide.at[array], out, out_sem.at[parts + array]))
        stores[-1].start()
    for load, store in zip(loads, stores):
        load.wait()
        store.start()
    for store in stores:
        store.wait()


def on_device(query, key_rows, value_rows, grad_out):
    tok, dh = key_rows.shape
    heads = query.shape[1] // dh
    blocks = REACH + 1
    vmem = pltpu.VMEM
    dma = pltpu.SemaphoreType.DMA
    grad_query, fin = pl.pallas_call(
        kernel,
        out_shape=(
            jax.ShapeDtypeStruct(query.shape, BF16),
            jax.ShapeDtypeStruct((2, tok, dh), BF16),
        ),
        in_specs=[pl.BlockSpec(memory_space=pl.ANY)] * 4,
        out_specs=(pl.BlockSpec(memory_space=pl.ANY),) * 2,
        scratch_shapes=[
            vmem((tok, heads * dh), BF16),
            vmem((tok, heads * dh), BF16),
            vmem((2, blocks * tok, dh), BF16),
            vmem((blocks, heads, tok, tok), F32),
            vmem((heads, blocks * tok, tok), F32),
            vmem((blocks, heads, 1, tok), F32),
            vmem((heads, 1, tok), F32),
            vmem((heads, 1, tok), F32),
            vmem((heads, 1, tok), F32),
            vmem((tok, heads * dh), BF16),
            vmem((2, 2, tok, dh), F32),
            vmem((blocks, tok, dh), BF16),
            vmem((blocks, tok, dh), BF16),
            vmem((3, tok, dh), F32),
            vmem((2, tok, dh), BF16),
            vmem((2, 2, tok // 2, dh), BF16),
            vmem((2, tok, dh), BF16),
            vmem((2, tok, dh), BF16),
            vmem((tok, dh), BF16),
            vmem((tok, dh), BF16),
            vmem((2, tok, dh), BF16),
            dma((4,)),
            dma((64,)),
            dma((blocks, 2)),
            dma((blocks, 2)),
            dma((blocks,)),
            dma((2, 2)),
            dma((2, 2)),
            dma((2,)),
            dma((2,)),
        ],
        compiler_params=pltpu.CompilerParams(
            collective_id=0, has_side_effects=True, vmem_limit_bytes=67043328
        ),
    )(query, grad_out, key_rows, value_rows)
    parts = 4
    anywhere = pl.BlockSpec(memory_space=pl.ANY)
    return pl.pallas_call(
        finish,
        out_shape=(
            jax.ShapeDtypeStruct(query.shape, BF16),
            jax.ShapeDtypeStruct((tok, dh), F32),
            jax.ShapeDtypeStruct((tok, dh), F32),
        ),
        in_specs=[anywhere] * 2,
        out_specs=(anywhere,) * 3,
        scratch_shapes=[
            vmem((parts, tok // parts, heads * dh), BF16),
            vmem((2, tok, dh), BF16),
            vmem((2, tok, dh), F32),
            dma((parts + 1,)),
            dma((parts + 2,)),
        ],
    )(grad_query, fin)


def solution(mesh):
    return jax.shard_map(
        on_device,
        mesh=mesh,
        in_specs=(P("seq", "head"), P("seq", None), P("seq", None), P("seq", "head")),
        out_specs=(P("seq", "head"), P("seq", None), P("seq", None)),
        check_vma=False,
    )
```

```python
import jax
import jax.numpy as jnp
from jax import lax
from jax.experimental import pallas as pl
from jax.experimental.pallas import tpu as pltpu
from jax.sharding import PartitionSpec as P

F32 = jnp.float32
BF16 = jnp.bfloat16
MESH = pl.DeviceIdType.MESH
REACH = 4
PIECES = 2
LOG2E = 1.4426950408889634
NEG = -1e30
NT = (((1,), (1,)), ((), ()))
NN = (((1,), (0,)), ((), ()))
TN = (((0,), (0,)), ((), ()))


def kernel(
    q_hbm, g_hbm, k_hbm, v_hbm,
    dq_ref, fin,
    q_ref, g_ref, kv, e_ref, ds_ref, md, m_run, l_run, dl_run,
    acc, pair_send, pair_recv, keep, odd_send, opp_recv, chain_send, chain_recv,
    fin_send, fin_recv,
    load_sem, send_sem, net_sem, mate_sem, pair_sem, opp_sem, chain_sem, across_sem, fin_sem,
):
    tok, dh = e_ref.shape[2], kv.shape[2]
    heads = e_ref.shape[1]
    hb = tok // 2
    sb = hb // PIECES
    blocks = REACH + 1
    scale = dh ** (-0.5)
    to_log2 = scale * LOG2E
    n_seq = lax.axis_size("seq")
    s, hd = lax.axis_index("seq"), lax.axis_index("head")
    xl, xh, c = lax.rem(s, 2), lax.div(hd, 2), lax.rem(hd, 2)
    opp = s + 1 - 2 * xl
    mate = (s, hd + 1 - 2 * c)
    across = (s, lax.rem(hd + 2, 4))

    def piece(index, sub):
        return pl.ds(pl.multiple_of(index * hb + sub * sb, sb), sb)

    loads = [
        pltpu.make_async_copy(src, dst, load_sem.at[i])
        for i, (src, dst) in enumerate(
            ((k_hbm, kv.at[0, :tok]), (v_hbm, kv.at[1, :tok]), (q_hbm, q_ref), (g_hbm, g_ref))
        )
    ]
    for load in loads:
        load.start()
    barrier = pltpu.get_barrier_semaphore()

    def greet(device):
        pl.semaphore_signal(barrier, inc=1, device_id=device, device_id_type=MESH)

    for head in (hd, across[1]):
        greet((opp, head))
    greet(mate)
    greet(across)

    @pl.when(s + 2 < n_seq)
    def _():
        greet((s + 2, hd))

    @pl.when(s >= 2)
    def _():
        greet((s - 2, hd))

    pl.semaphore_wait(barrier, 4 + jnp.minimum(n_seq - 1 - s, 2) // 2 + jnp.minimum(s, 2) // 2)
    for load in loads[:2]:
        load.wait()

    pending = []

    def send(cond, src, dst, recv_sem, device):
        sem = send_sem.at[len(pending)]
        pending.append((cond, src.shape[0]))

        @pl.when(cond())
        def _():
            pltpu.make_async_remote_copy(
                src_ref=src, dst_ref=dst, send_sem=sem, recv_sem=recv_sem,
                device_id=device, device_id_type=MESH,
            ).start()

    def wait_sent():
        for i, (cond, size) in enumerate(pending):
            @pl.when(cond())
            def _(i=i, size=size):
                buf = pair_send.at[0, :size]
                pltpu.make_async_remote_copy(
                    src_ref=buf, dst_ref=buf, send_sem=send_sem.at[i], recv_sem=fin_sem.at[0],
                    device_id=mate, device_id_type=MESH,
                ).wait_send()

    def arrived(buf, sem):
        pltpu.make_async_remote_copy(
            src_ref=buf, dst_ref=buf, send_sem=send_sem.at[0], recv_sem=sem,
            device_id=mate, device_id_type=MESH,
        ).wait_recv()

    def when_arrived(cond, buf, sem):
        @pl.when(cond())
        def _():
            arrived(buf, sem)

    def kv_half(d, array, index):
        return kv.at[array, pl.ds(pl.multiple_of(d * tok + index * hb, hb), hb), :]

    def kv_piece(d, array, index, sub):
        return kv.at[array, pl.ds(pl.multiple_of(d * tok + index * hb + sub * sb, sb), sb), :]

    def over_x(cond, src_slot, dst_slot, sub):
        for x_hi in range(2):
            send(
                cond, kv_piece(src_slot, c, xh, sub), kv_piece(dst_slot, c, xh, sub),
                net_sem.at[dst_slot, xh, sub], (opp, 2 * x_hi + c),
            )

    def to_mate(cond, d, index):
        send(cond, kv_half(d, c, index), kv_half(d, c, index), mate_sem.at[d, index], mate)

    order = (xh, 1 - xh)
    for index in order:
        for sub in range(PIECES):
            send(
                lambda: s + 2 < n_seq, kv_piece(0, c, index, sub), kv_piece(2, c, index, sub),
                net_sem.at[2, index, sub], (s + 2, hd),
            )
            if index is order[0]:
                over_x(lambda: xl == 0, 0, 1, sub)

    def relay_two(j, parity=None):
        def here():
            return (s >= 2) if parity is None else (s >= 2) & (xl == parity)

        index = order[j]
        for sub in range(PIECES):
            when_arrived(here, kv_piece(2, c, index, sub), net_sem.at[2, index, sub])
            send(
                lambda: here() & (s + 2 < n_seq), kv_piece(2, c, index, sub), kv_piece(4, c, index, sub),
                net_sem.at[4, index, sub], (s + 2, hd),
            )
            if j == 0:
                over_x(here, 2, 3 - 2 * xl, sub)
        to_mate(here, 2, index)

    def relay_four(j, parity=None):
        def here():
            return (s >= 4) if parity is None else (s >= 4) & (xl == parity)

        index = order[j]
        for sub in range(PIECES):
            when_arrived(here, kv_piece(4, c, index, sub), net_sem.at[4, index, sub])
            if j == 0:
                over_x(lambda: here() & (xl == 1), 4, 3, sub)
        to_mate(here, 4, index)

    def relay_odd(cond, d):
        for index in range(2):
            for sub in range(PIECES):
                when_arrived(cond, kv_piece(d, c, index, sub), net_sem.at[d, index, sub])
            to_mate(cond, d, index)

    def mate_ready(d):
        for index in range(2):
            arrived(kv_half(d, 1 - c, index), mate_sem.at[d, index])

    def key_range(d, qc):
        if d == 0:
            return 0, hb * (qc + 1)
        if d == REACH:
            return hb * qc, tok
        return 0, tok

    def query_range(d, kc):
        if d == 0:
            return hb * kc, tok
        if d == REACH:
            return 0, hb * (kc + 1)
        return 0, tok

    def rows_of(d, k0, k1):
        return pl.ds(pl.multiple_of(d * tok + k0, hb), k1 - k0)

    def run_hooks(h, hooks):
        for at, steps in hooks.items():
            @pl.when(h == at)
            def _(steps=steps):
                for step in steps:
                    step()

    def scores_of(d, kind):
        for h in range(heads):
            cols = slice(h * dh, (h + 1) * dh)
            for qc in range(2):
                k0, k1 = key_range(kind, qc)
                rows = rows_of(d, k0, k1)
                qs = slice(qc * hb, (qc + 1) * hb)
                logits = to_log2 * lax.dot_general(
                    kv[0, rows, :], q_ref[qs, cols], NT, preferred_element_type=F32
                )
                dprobs = lax.dot_general(
                    kv[1, rows, :], g_ref[qs, cols], NT, preferred_element_type=F32
                )
                if kind in (0, REACH):
                    row = lax.broadcasted_iota(jnp.int32, logits.shape, 0) + k0
                    col = lax.broadcasted_iota(jnp.int32, logits.shape, 1) + qc * hb
                    logits = jnp.where((row <= col) if kind == 0 else (row > col), logits, NEG)
                top = jnp.max(logits, axis=0, keepdims=True)
                if kind:
                    before = m_run[h, :, qs]
                    top = jnp.maximum(before, top)
                expo = jnp.exp2(logits - top)
                total = jnp.sum(expo, axis=0, keepdims=True)
                dots = jnp.sum(expo * dprobs, axis=0, keepdims=True)
                e_ref[d, h, k0:k1, qs] = expo
                ds_ref[h, rows, qs] = dprobs
                md[d, h, :, qs] = top
                if kind:
                    fade = jnp.exp2(before - top)
                    total += l_run[h, :, qs] * fade
                    dots += dl_run[h, :, qs] * fade
                m_run[h, :, qs] = top
                l_run[h, :, qs] = total
                dl_run[h, :, qs] = dots

    for load in loads[2:]:
        load.wait()
    scores_of(0, 0)
    for d in range(1, REACH + 1):
        @pl.when(s < d)
        def _(d=d):
            kv[0, d * tok : (d + 1) * tok, :] = jnp.zeros((tok, dh), BF16)
            for h in range(heads):
                ds_ref[h, d * tok : (d + 1) * tok, :] = jnp.zeros((tok, tok), F32)

    relay_two(0)
    relay_two(1, 0)
    relay_odd(lambda: xl == 1, 1)
    first, second = 2 - xl, 1 + xl

    @pl.when(s >= first)
    def _():
        mate_ready(first)
        scores_of(first, 1)

    relay_two(1, 1)
    relay_odd(lambda: (xl == 0) & (s >= 1), 1)
    relay_four(0, 0)

    @pl.when(s >= second)
    def _():
        mate_ready(second)
        scores_of(second, 1)

    relay_four(0, 1)
    relay_odd(lambda: (xl == 1) & (s >= 3), 3)
    relay_four(1)
    relay_odd(lambda: (xl == 0) & (s >= 3), 3)

    @pl.when(s >= 4)
    def _():
        mate_ready(4)
        scores_of(4, 4)

    @pl.when(s >= 3)
    def _():
        mate_ready(3)
        scores_of(3, 3)

    inverse = 1.0 / l_run[...]
    dl_run[...] = dl_run[...] * inverse
    l_run[...] = inverse

    def grads_of(d, into):
        for kc in range(2):
            q0, q1 = query_range(d, kc)
            ks, qs = slice(kc * hb, (kc + 1) * hb), slice(q0, q1)
            rows = slice(d * tok + kc * hb, d * tok + (kc + 1) * hb)
            for h in range(heads):
                cols = slice(h * dh, (h + 1) * dh)
                weight = jnp.exp2(md[d, h, :, qs] - m_run[h, :, qs]) * l_run[h, :, qs]
                probs = e_ref[d, h, ks, qs] * weight
                dscores = probs * (ds_ref[h, rows, qs] - dl_run[h, :, qs])
                ds_ref[h, rows, qs] = dscores
                to_value = lax.dot_general(
                    probs.astype(BF16), g_ref[qs, cols], NN, preferred_element_type=F32
                )
                to_key = lax.dot_general(
                    dscores.astype(BF16), q_ref[qs, cols], NN, preferred_element_type=F32
                )
                if h:
                    to_value += acc[into, 1, ks, :]
                    to_key += acc[into, 0, ks, :]
                acc[into, 1, ks, :] = to_value
                acc[into, 0, ks, :] = to_key * scale if h == heads - 1 else to_key

    def query_grads(hooks):
        def body(h, carry):
            run_hooks(h, hooks)
            cols = pl.ds(pl.multiple_of(h * dh, dh), dh)
            for qc in range(2):
                qs = slice(qc * hb, (qc + 1) * hb)
                total = 0.0
                edge = (REACH * tok) if qc == 0 else (REACH * tok + hb)
                spans = ((0, hb), (tok, blocks * tok)) if qc == 0 else ((0, REACH * tok), (edge, blocks * tok))
                for r0, r1 in spans:
                    total += lax.dot_general(
                        ds_ref[h, r0:r1, qs].astype(BF16), kv[0, r0:r1, :], TN, preferred_element_type=F32
                    )
                dq_ref[qs, cols] = (total * scale).astype(BF16)
            return carry

        lax.fori_loop(0, heads, body, 0)

    def pair_out(d):
        @pl.when(s >= d)
        def _():
            pair_send[d] = acc[place[d], 1 - c].astype(BF16)

        send(lambda: s >= d, pair_send.at[d], pair_recv.at[d], pair_sem.at[d], mate)

    def odd_out(d):
        o = d // 2

        @pl.when(s >= d)
        def _():
            arrived(pair_recv.at[d], pair_sem.at[d])
            odd_send[o] = (acc[place[d], c] + pair_recv[d].astype(F32)).astype(BF16)

        for sub in range(PIECES):
            for x_hi in range(2):
                r0 = x_hi * hb + sub * sb
                send(
                    lambda: s >= d, odd_send.at[o, r0 : r0 + sb], opp_recv.at[o, xh, sub],
                    opp_sem.at[o, xh, sub], (opp, 2 * x_hi + c),
                )

    def base(d):
        @pl.when(s >= d)
        def _():
            arrived(pair_recv.at[d], pair_sem.at[d])
            keep[d // 2] = acc[place[d], c] + pair_recv[d].astype(F32)

    def add_opp(o, sub):
        @pl.when(s >= 2 * o + 2 * xl)
        def _():
            for x_hi in range(2):
                arrived(opp_recv.at[o, x_hi, sub], opp_sem.at[o, x_hi, sub])
            keep[o + xl, piece(xh, sub), :] += opp_recv[o, 0, sub].astype(F32) + opp_recv[o, 1, sub].astype(F32)

    def add_chain(i, index, sub):
        @pl.when((s >= 2 - 2 * i) & (s + 2 < n_seq))
        def _():
            rows = piece(index, sub)
            arrived(chain_recv.at[i, rows, :], chain_sem.at[i, index, sub])
            keep[1 - i, rows, :] += chain_recv[i, rows, :].astype(F32)

    def chain_out(i, index, sub, parity=None):
        def here():
            some = s >= 4 - 2 * i
            return some if parity is None else some & (xl == parity)

        rows = piece(index, sub)

        @pl.when(here())
        def _():
            chain_send[i, rows, :] = keep[2 - i, rows, :].astype(BF16)

        send(
            here, chain_send.at[i, rows, :], chain_recv.at[i, rows, :], chain_sem.at[i, index, sub],
            (s - 2, hd),
        )

    def first_chain():
        base(4)
        for sub in range(PIECES):
            chain_out(0, 1 - xh, sub)
        for sub in range(PIECES):
            chain_out(0, xh, sub, 0)

    def second_base():
        base(2)

    def last_of_four():
        for sub in range(PIECES):
            add_opp(1, sub)
            chain_out(0, xh, sub, 1)

    def early_two():
        for sub in range(PIECES):
            add_chain(0, 1 - xh, sub)
            chain_out(1, 1 - xh, sub)

    steps = ((3, None), (4, lambda: odd_out(3)), (1, first_chain), (2, lambda: odd_out(1)), (0, second_base))
    place = {d: i % 2 for i, (d, _) in enumerate(steps)}
    for d, after in steps:
        @pl.when(s >= d)
        def _(d=d):
            grads_of(d, place[d])

        pair_out(d)
        if after is not None:
            after()
    query_grads({0: [last_of_four], 1: [lambda: base(0)], 2: [early_two]})
    for sub in range(PIECES):
        add_opp(0, sub)
        add_chain(0, xh, sub)
        chain_out(1, xh, sub)
    always = lambda: s >= 0
    for index in (1 - xh, xh):
        for sub in range(PIECES):
            rows = piece(index, sub)
            add_chain(1, index, sub)
            fin_send[rows, :] = keep[0, rows, :].astype(BF16)
            send(always, fin_send.at[rows, :], fin_recv.at[rows, :], across_sem.at[index, sub], across)
    for index in (xh, 1 - xh):
        for sub in range(PIECES):
            rows = piece(index, sub)
            arrived(fin_recv.at[rows, :], across_sem.at[index, sub])
            fin[c, rows, :] = (fin_send[rows, :].astype(F32) + fin_recv[rows, :].astype(F32)).astype(BF16)
            send(always, fin.at[c, rows, :], fin.at[c, rows, :], fin_sem.at[index, sub], mate)
    for index in (xh, 1 - xh):
        for sub in range(PIECES):
            arrived(fin.at[1 - c, piece(index, sub), :], fin_sem.at[index, sub])
    wait_sent()


def finish(dq_in, fin_in, dq_out, dk_out, dv_out, wide, sem):
    stores = [pltpu.make_async_copy(dq_in, dq_out, sem.at[2])]
    stores[0].start()
    for array, out in enumerate((dk_out, dv_out)):
        wide[array] = fin_in[array].astype(F32)
        stores.append(pltpu.make_async_copy(wide.at[array], out, sem.at[array]))
        stores[-1].start()
    for store in stores:
        store.wait()


def on_device(query, key_rows, value_rows, grad_out):
    tok, dh = key_rows.shape
    heads = query.shape[1] // dh
    blocks = REACH + 1
    vmem = pltpu.VMEM
    dma = pltpu.SemaphoreType.DMA
    grad_query, fin = pl.pallas_call(
        kernel,
        out_shape=(
            vmem(query.shape, BF16),
            vmem((2, tok, dh), BF16),
        ),
        in_specs=[pl.BlockSpec(memory_space=pl.ANY)] * 4,
        out_specs=(pl.BlockSpec(memory_space=vmem),) * 2,
        scratch_shapes=[
            vmem((tok, heads * dh), BF16),
            vmem((tok, heads * dh), BF16),
            vmem((2, blocks * tok, dh), BF16),
            vmem((blocks, heads, tok, tok), F32),
            vmem((heads, blocks * tok, tok), F32),
            vmem((blocks, heads, 1, tok), F32),
            vmem((heads, 1, tok), F32),
            vmem((heads, 1, tok), F32),
            vmem((heads, 1, tok), F32),
            vmem((2, 2, tok, dh), F32),
            vmem((blocks, tok, dh), BF16),
            vmem((blocks, tok, dh), BF16),
            vmem((3, tok, dh), F32),
            vmem((2, tok, dh), BF16),
            vmem((2, 2, PIECES, tok // 2 // PIECES, dh), BF16),
            vmem((2, tok, dh), BF16),
            vmem((2, tok, dh), BF16),
            vmem((tok, dh), BF16),
            vmem((tok, dh), BF16),
            dma((4,)),
            dma((128,)),
            dma((blocks, 2, PIECES)),
            dma((blocks, 2)),
            dma((blocks,)),
            dma((2, 2, PIECES)),
            dma((2, 2, PIECES)),
            dma((2, PIECES)),
            dma((2, PIECES)),
        ],
        compiler_params=pltpu.CompilerParams(
            collective_id=0, has_side_effects=True, vmem_limit_bytes=65400000
        ),
    )(query, grad_out, key_rows, value_rows)
    anywhere = pl.BlockSpec(memory_space=pl.ANY)
    return pl.pallas_call(
        finish,
        out_shape=(
            jax.ShapeDtypeStruct(query.shape, BF16),
            jax.ShapeDtypeStruct((tok, dh), F32),
            jax.ShapeDtypeStruct((tok, dh), F32),
        ),
        in_specs=[pl.BlockSpec(memory_space=vmem)] * 2,
        out_specs=(anywhere,) * 3,
        scratch_shapes=[vmem((2, tok, dh), F32), dma((3,))],
        compiler_params=pltpu.CompilerParams(vmem_limit_bytes=8 << 20),
    )(grad_query, fin)


def solution(mesh):
    return jax.shard_map(
        on_device,
        mesh=mesh,
        in_specs=(P("seq", "head"), P("seq", None), P("seq", None), P("seq", "head")),
        out_specs=(P("seq", "head"), P("seq", None), P("seq", None)),
        check_vma=False,
    )
```

```python
import jax
import jax.numpy as jnp
from jax import lax
from jax.experimental import pallas as pl
from jax.experimental.pallas import tpu as pltpu
from jax.sharding import PartitionSpec as P

F32 = jnp.float32
BF16 = jnp.bfloat16
MESH = pl.DeviceIdType.MESH
REACH = 4
PIECES = 2
LOG2E = 1.4426950408889634
NEG = -1e30
NT = (((1,), (1,)), ((), ()))
NN = (((1,), (0,)), ((), ()))
TN = (((0,), (0,)), ((), ()))


def kernel(
    q_hbm, g_hbm, k_hbm, v_hbm,
    dq_ref, fin,
    q_ref, g_ref, kv, e_ref, ds_ref, md, m_run, l_run, dl_run,
    acc, pair_send, pair_recv, keep, odd_send, opp_recv, chain_send, chain_recv,
    fin_send, fin_recv,
    load_sem, send_sem, net_sem, mate_sem, pair_sem, opp_sem, chain_sem, across_sem, fin_sem,
):
    tok, dh = e_ref.shape[2], kv.shape[2]
    heads = e_ref.shape[1]
    hb = tok // 2
    sb = hb // PIECES
    blocks = REACH + 1
    scale = dh ** (-0.5)
    to_log2 = scale * LOG2E
    n_seq = lax.axis_size("seq")
    s, hd = lax.axis_index("seq"), lax.axis_index("head")
    xl, xh, c = lax.rem(s, 2), lax.div(hd, 2), lax.rem(hd, 2)
    opp = s + 1 - 2 * xl
    mate = (s, hd + 1 - 2 * c)
    across = (s, lax.rem(hd + 2, 4))

    def piece(index, sub):
        return pl.ds(pl.multiple_of(index * hb + sub * sb, sb), sb)

    loads = [
        pltpu.make_async_copy(src, dst, load_sem.at[i])
        for i, (src, dst) in enumerate(
            ((k_hbm, kv.at[0, :tok]), (v_hbm, kv.at[1, :tok]), (q_hbm, q_ref), (g_hbm, g_ref))
        )
    ]
    for load in loads:
        load.start()
    barrier = pltpu.get_barrier_semaphore()

    def greet(device):
        pl.semaphore_signal(barrier, inc=1, device_id=device, device_id_type=MESH)

    for head in (hd, across[1]):
        greet((opp, head))
    greet(mate)
    greet(across)

    @pl.when(s + 2 < n_seq)
    def _():
        greet((s + 2, hd))

    @pl.when(s >= 2)
    def _():
        greet((s - 2, hd))

    pl.semaphore_wait(barrier, 4 + jnp.minimum(n_seq - 1 - s, 2) // 2 + jnp.minimum(s, 2) // 2)
    for load in loads[:2]:
        load.wait()

    pending = []

    def send(cond, src, dst, recv_sem, device):
        sem = send_sem.at[len(pending)]
        pending.append((cond, src.shape[0]))

        @pl.when(cond())
        def _():
            pltpu.make_async_remote_copy(
                src_ref=src, dst_ref=dst, send_sem=sem, recv_sem=recv_sem,
                device_id=device, device_id_type=MESH,
            ).start()

    def wait_sent():
        for i, (cond, size) in enumerate(pending):
            @pl.when(cond())
            def _(i=i, size=size):
                buf = pair_send.at[0, :size]
                pltpu.make_async_remote_copy(
                    src_ref=buf, dst_ref=buf, send_sem=send_sem.at[i], recv_sem=fin_sem.at[0],
                    device_id=mate, device_id_type=MESH,
                ).wait_send()

    def arrived(buf, sem):
        pltpu.make_async_remote_copy(
            src_ref=buf, dst_ref=buf, send_sem=send_sem.at[0], recv_sem=sem,
            device_id=mate, device_id_type=MESH,
        ).wait_recv()

    def when_arrived(cond, buf, sem):
        @pl.when(cond())
        def _():
            arrived(buf, sem)

    def kv_half(d, array, index):
        return kv.at[array, pl.ds(pl.multiple_of(d * tok + index * hb, hb), hb), :]

    def kv_piece(d, array, index, sub):
        return kv.at[array, pl.ds(pl.multiple_of(d * tok + index * hb + sub * sb, sb), sb), :]

    def over_x(cond, src_slot, dst_slot, sub):
        for x_hi in range(2):
            send(
                cond, kv_piece(src_slot, c, xh, sub), kv_piece(dst_slot, c, xh, sub),
                net_sem.at[dst_slot, xh, sub], (opp, 2 * x_hi + c),
            )

    def to_mate(cond, d, index):
        send(cond, kv_half(d, c, index), kv_half(d, c, index), mate_sem.at[d, index], mate)

    order = (xh, 1 - xh)
    for index in order:
        for sub in range(PIECES):
            send(
                lambda: s + 2 < n_seq, kv_piece(0, c, index, sub), kv_piece(2, c, index, sub),
                net_sem.at[2, index, sub], (s + 2, hd),
            )
            if index is order[0]:
                over_x(lambda: xl == 0, 0, 1, sub)

    def relay_two(j, parity=None):
        def here():
            return (s >= 2) if parity is None else (s >= 2) & (xl == parity)

        index = order[j]
        for sub in range(PIECES):
            when_arrived(here, kv_piece(2, c, index, sub), net_sem.at[2, index, sub])
            send(
                lambda: here() & (s + 2 < n_seq), kv_piece(2, c, index, sub), kv_piece(4, c, index, sub),
                net_sem.at[4, index, sub], (s + 2, hd),
            )
            if j == 0:
                over_x(here, 2, 3 - 2 * xl, sub)
        to_mate(here, 2, index)

    def relay_four(j, parity=None):
        def here():
            return (s >= 4) if parity is None else (s >= 4) & (xl == parity)

        index = order[j]
        for sub in range(PIECES):
            when_arrived(here, kv_piece(4, c, index, sub), net_sem.at[4, index, sub])
            if j == 0:
                over_x(lambda: here() & (xl == 1), 4, 3, sub)
        to_mate(here, 4, index)

    def relay_odd(cond, d):
        for index in range(2):
            for sub in range(PIECES):
                when_arrived(cond, kv_piece(d, c, index, sub), net_sem.at[d, index, sub])
            to_mate(cond, d, index)

    def mate_ready(d):
        for index in range(2):
            arrived(kv_half(d, 1 - c, index), mate_sem.at[d, index])

    def key_range(d, qc):
        if d == 0:
            return 0, hb * (qc + 1)
        if d == REACH:
            return hb * qc, tok
        return 0, tok

    def query_range(d, kc):
        if d == 0:
            return hb * kc, tok
        if d == REACH:
            return 0, hb * (kc + 1)
        return 0, tok

    def rows_of(d, k0, k1):
        return pl.ds(pl.multiple_of(d * tok + k0, hb), k1 - k0)

    def run_hooks(h, hooks):
        for at, steps in hooks.items():
            @pl.when(h == at)
            def _(steps=steps):
                for step in steps:
                    step()

    def scores_of(d, kind):
        for h in range(heads):
            cols = slice(h * dh, (h + 1) * dh)
            for qc in range(2):
                k0, k1 = key_range(kind, qc)
                rows = rows_of(d, k0, k1)
                qs = slice(qc * hb, (qc + 1) * hb)
                logits = to_log2 * lax.dot_general(
                    kv[0, rows, :], q_ref[qs, cols], NT, preferred_element_type=F32
                )
                dprobs = lax.dot_general(
                    kv[1, rows, :], g_ref[qs, cols], NT, preferred_element_type=F32
                )
                if kind in (0, REACH):
                    row = lax.broadcasted_iota(jnp.int32, logits.shape, 0) + k0
                    col = lax.broadcasted_iota(jnp.int32, logits.shape, 1) + qc * hb
                    logits = jnp.where((row <= col) if kind == 0 else (row > col), logits, NEG)
                top = jnp.max(logits, axis=0, keepdims=True)
                if kind:
                    before = m_run[h, :, qs]
                    top = jnp.maximum(before, top)
                expo = jnp.exp2(logits - top)
                total = jnp.sum(expo, axis=0, keepdims=True)
                dots = jnp.sum(expo * dprobs, axis=0, keepdims=True)
                e_ref[d, h, k0:k1, qs] = expo
                ds_ref[h, rows, qs] = dprobs
                md[d, h, :, qs] = top
                if kind:
                    fade = jnp.exp2(before - top)
                    total += l_run[h, :, qs] * fade
                    dots += dl_run[h, :, qs] * fade
                m_run[h, :, qs] = top
                l_run[h, :, qs] = total
                dl_run[h, :, qs] = dots

    for load in loads[2:]:
        load.wait()
    scores_of(0, 0)
    for d in range(1, REACH + 1):
        @pl.when(s < d)
        def _(d=d):
            kv[0, d * tok : (d + 1) * tok, :] = jnp.zeros((tok, dh), BF16)
            for h in range(heads):
                ds_ref[h, d * tok : (d + 1) * tok, :] = jnp.zeros((tok, tok), F32)

    relay_two(0)
    relay_two(1, 0)
    relay_odd(lambda: xl == 1, 1)
    first, second = 2 - xl, 1 + xl

    @pl.when(s >= first)
    def _():
        mate_ready(first)
        scores_of(first, 1)

    relay_two(1, 1)
    relay_odd(lambda: (xl == 0) & (s >= 1), 1)
    relay_four(0, 0)

    @pl.when(s >= second)
    def _():
        mate_ready(second)
        scores_of(second, 1)

    relay_four(0, 1)
    relay_odd(lambda: (xl == 1) & (s >= 3), 3)
    relay_four(1)
    relay_odd(lambda: (xl == 0) & (s >= 3), 3)

    @pl.when(s >= 4)
    def _():
        mate_ready(4)
        scores_of(4, 4)

    @pl.when(s >= 3)
    def _():
        mate_ready(3)
        scores_of(3, 3)

    inverse = 1.0 / l_run[...]
    dl_run[...] = dl_run[...] * inverse
    l_run[...] = inverse

    def grads_of(d, into):
        for kc in range(2):
            q0, q1 = query_range(d, kc)
            ks, qs = slice(kc * hb, (kc + 1) * hb), slice(q0, q1)
            rows = slice(d * tok + kc * hb, d * tok + (kc + 1) * hb)
            for h in range(heads):
                cols = slice(h * dh, (h + 1) * dh)
                weight = jnp.exp2(md[d, h, :, qs] - m_run[h, :, qs]) * l_run[h, :, qs]
                probs = e_ref[d, h, ks, qs] * weight
                dscores = probs * (ds_ref[h, rows, qs] - dl_run[h, :, qs])
                ds_ref[h, rows, qs] = dscores
                to_value = lax.dot_general(
                    probs.astype(BF16), g_ref[qs, cols], NN, preferred_element_type=F32
                )
                to_key = lax.dot_general(
                    dscores.astype(BF16), q_ref[qs, cols], NN, preferred_element_type=F32
                )
                if h:
                    to_value += acc[into, 1, ks, :]
                    to_key += acc[into, 0, ks, :]
                acc[into, 1, ks, :] = to_value
                acc[into, 0, ks, :] = to_key * scale if h == heads - 1 else to_key

    def query_grads(hooks):
        def body(h, carry):
            run_hooks(h, hooks)
            cols = pl.ds(pl.multiple_of(h * dh, dh), dh)
            for qc in range(2):
                qs = slice(qc * hb, (qc + 1) * hb)
                total = 0.0
                edge = (REACH * tok) if qc == 0 else (REACH * tok + hb)
                spans = ((0, hb), (tok, blocks * tok)) if qc == 0 else ((0, REACH * tok), (edge, blocks * tok))
                for r0, r1 in spans:
                    total += lax.dot_general(
                        ds_ref[h, r0:r1, qs].astype(BF16), kv[0, r0:r1, :], TN, preferred_element_type=F32
                    )
                dq_ref[qs, cols] = (total * scale).astype(BF16)
            return carry

        lax.fori_loop(0, heads, body, 0)

    def pair_out(d):
        @pl.when(s >= d)
        def _():
            pair_send[d] = acc[place[d], 1 - c].astype(BF16)

        send(lambda: s >= d, pair_send.at[d], pair_recv.at[d], pair_sem.at[d], mate)

    def odd_out(d):
        o = d // 2

        @pl.when(s >= d)
        def _():
            arrived(pair_recv.at[d], pair_sem.at[d])
            odd_send[o] = (acc[place[d], c] + pair_recv[d].astype(F32)).astype(BF16)

        for sub in range(PIECES):
            for x_hi in range(2):
                r0 = x_hi * hb + sub * sb
                send(
                    lambda: s >= d, odd_send.at[o, r0 : r0 + sb], opp_recv.at[o, xh, sub],
                    opp_sem.at[o, xh, sub], (opp, 2 * x_hi + c),
                )

    def base(d):
        @pl.when(s >= d)
        def _():
            arrived(pair_recv.at[d], pair_sem.at[d])
            keep[d // 2] = acc[place[d], c] + pair_recv[d].astype(F32)

    def add_opp(o, sub):
        @pl.when(s >= 2 * o + 2 * xl)
        def _():
            for x_hi in range(2):
                arrived(opp_recv.at[o, x_hi, sub], opp_sem.at[o, x_hi, sub])
            keep[o + xl, piece(xh, sub), :] += opp_recv[o, 0, sub].astype(F32) + opp_recv[o, 1, sub].astype(F32)

    def add_chain(i, index, sub):
        @pl.when((s >= 2 - 2 * i) & (s + 2 < n_seq))
        def _():
            rows = piece(index, sub)
            arrived(chain_recv.at[i, rows, :], chain_sem.at[i, index, sub])
            keep[1 - i, rows, :] += chain_recv[i, rows, :].astype(F32)

    def chain_out(i, index, sub, parity=None):
        def here():
            some = s >= 4 - 2 * i
            return some if parity is None else some & (xl == parity)

        rows = piece(index, sub)

        @pl.when(here())
        def _():
            chain_send[i, rows, :] = keep[2 - i, rows, :].astype(BF16)

        send(
            here, chain_send.at[i, rows, :], chain_recv.at[i, rows, :], chain_sem.at[i, index, sub],
            (s - 2, hd),
        )

    def first_chain():
        base(4)
        for sub in range(PIECES):
            chain_out(0, 1 - xh, sub)
        for sub in range(PIECES):
            chain_out(0, xh, sub, 0)

    def second_base():
        base(2)

    def last_of_four():
        for sub in range(PIECES):
            add_opp(1, sub)
            chain_out(0, xh, sub, 1)

    def early_two():
        for sub in range(PIECES):
            add_chain(0, 1 - xh, sub)
            chain_out(1, 1 - xh, sub)

    steps = ((3, None), (4, lambda: odd_out(3)), (1, first_chain), (2, lambda: odd_out(1)), (0, second_base))
    place = {d: i % 2 for i, (d, _) in enumerate(steps)}
    for d, after in steps:
        @pl.when(s >= d)
        def _(d=d):
            grads_of(d, place[d])

        pair_out(d)
        if after is not None:
            after()
    query_grads({0: [last_of_four], 1: [early_two], 3: [lambda: base(0)]})
    for sub in range(PIECES):
        add_opp(0, sub)
        add_chain(0, xh, sub)
        chain_out(1, xh, sub)
    always = lambda: s >= 0
    for index in (1 - xh, xh):
        for sub in range(PIECES):
            rows = piece(index, sub)
            add_chain(1, index, sub)
            fin_send[rows, :] = keep[0, rows, :].astype(BF16)
            send(always, fin_send.at[rows, :], fin_recv.at[rows, :], across_sem.at[index, sub], across)
    for index in (xh, 1 - xh):
        for sub in range(PIECES):
            rows = piece(index, sub)
            arrived(fin_recv.at[rows, :], across_sem.at[index, sub])
            fin[c, rows, :] = (fin_send[rows, :].astype(F32) + fin_recv[rows, :].astype(F32)).astype(BF16)
            send(always, fin.at[c, rows, :], fin.at[c, rows, :], fin_sem.at[index, sub], mate)
    for index in (xh, 1 - xh):
        for sub in range(PIECES):
            arrived(fin.at[1 - c, piece(index, sub), :], fin_sem.at[index, sub])
    wait_sent()


def finish(dq_in, fin_in, dq_out, dk_out, dv_out, wide, sem):
    stores = [pltpu.make_async_copy(dq_in, dq_out, sem.at[2])]
    stores[0].start()
    for array, out in enumerate((dk_out, dv_out)):
        wide[array] = fin_in[array].astype(F32)
        stores.append(pltpu.make_async_copy(wide.at[array], out, sem.at[array]))
        stores[-1].start()
    for store in stores:
        store.wait()


def on_device(query, key_rows, value_rows, grad_out):
    tok, dh = key_rows.shape
    heads = query.shape[1] // dh
    blocks = REACH + 1
    vmem = pltpu.VMEM
    dma = pltpu.SemaphoreType.DMA
    grad_query, fin = pl.pallas_call(
        kernel,
        out_shape=(
            vmem(query.shape, BF16),
            vmem((2, tok, dh), BF16),
        ),
        in_specs=[pl.BlockSpec(memory_space=pl.ANY)] * 4,
        out_specs=(pl.BlockSpec(memory_space=vmem),) * 2,
        scratch_shapes=[
            vmem((tok, heads * dh), BF16),
            vmem((tok, heads * dh), BF16),
            vmem((2, blocks * tok, dh), BF16),
            vmem((blocks, heads, tok, tok), F32),
            vmem((heads, blocks * tok, tok), F32),
            vmem((blocks, heads, 1, tok), F32),
            vmem((heads, 1, tok), F32),
            vmem((heads, 1, tok), F32),
            vmem((heads, 1, tok), F32),
            vmem((2, 2, tok, dh), F32),
            vmem((blocks, tok, dh), BF16),
            vmem((blocks, tok, dh), BF16),
            vmem((3, tok, dh), F32),
            vmem((2, tok, dh), BF16),
            vmem((2, 2, PIECES, tok // 2 // PIECES, dh), BF16),
            vmem((2, tok, dh), BF16),
            vmem((2, tok, dh), BF16),
            vmem((tok, dh), BF16),
            vmem((tok, dh), BF16),
            dma((4,)),
            dma((128,)),
            dma((blocks, 2, PIECES)),
            dma((blocks, 2)),
            dma((blocks,)),
            dma((2, 2, PIECES)),
            dma((2, 2, PIECES)),
            dma((2, PIECES)),
            dma((2, PIECES)),
        ],
        compiler_params=pltpu.CompilerParams(
            collective_id=0, has_side_effects=True, vmem_limit_bytes=65400000
        ),
    )(query, grad_out, key_rows, value_rows)
    anywhere = pl.BlockSpec(memory_space=pl.ANY)
    return pl.pallas_call(
        finish,
        out_shape=(
            jax.ShapeDtypeStruct(query.shape, BF16),
            jax.ShapeDtypeStruct((tok, dh), F32),
            jax.ShapeDtypeStruct((tok, dh), F32),
        ),
        in_specs=[pl.BlockSpec(memory_space=vmem)] * 2,
        out_specs=(anywhere,) * 3,
        scratch_shapes=[vmem((2, tok, dh), F32), dma((3,))],
        compiler_params=pltpu.CompilerParams(vmem_limit_bytes=8 << 20),
    )(grad_query, fin)


def solution(mesh):
    return jax.shard_map(
        on_device,
        mesh=mesh,
        in_specs=(P("seq", "head"), P("seq", None), P("seq", None), P("seq", "head")),
        out_specs=(P("seq", "head"), P("seq", None), P("seq", None)),
        check_vma=False,
    )
```
